512 devices in a mesh: gx: 32 (over y, x), gy: 16 (over z, core).
Axes of the slice: x: 4, y: 8, z: 8, core: 2. Of those that a mesh axis runs over, the one named last changes fastest.
Arguments:
- water_head: float32 [1024, 512, 128], P('gx', 'gy'), may hold values from -4 to 4
- conductivity: float32 [1024, 512, 128], P('gx', 'gy'), may hold values from 1 to 8
- recharge: float32 [1024, 512, 128], P('gx', 'gy'), may hold values from -4 to 4
Outputs:
- next_head: float32 [1024, 512, 128], P('gx', 'gy')
The draws below stay inside these ranges and needn't reach their ends.
All inputs are finite; a program needn't handle non-finite values.
Results may differ from the reference program's by a relative error of at most 0.008.
Values sent between devices are 32-bit elements; how exact they have to be, the bound alone decides.
No kernel may reach another device: no remote copies, remote signals or barrier semaphores. Data moves between devices by JAX's collectives and lax.ppermute only.
A program may use at most 64 MiB of HBM per device.

```python
import math
import jax
import jax.numpy as jnp
from jax import lax

COEF_Z = 8
COEF_X = 5120
COEF_Y = 5120
NX = 1024
NY = 512
NZ = 128


def modal_pattern(key):
    subkeys = jax.random.split(key, 5)
    waves_first = jax.random.randint(subkeys[0], (4,), 1, 9)
    waves_second = jax.random.randint(subkeys[1], (4,), 1, 9)
    waves_third = jax.random.randint(subkeys[2], (4,), 0, 4)
    phases = jax.random.uniform(subkeys[3], (4, 3), jnp.float32, -math.pi, math.pi)
    amplitudes = jax.random.uniform(subkeys[4], (4,), jnp.float32, -0.5, 0.5)
    coord_first = (jnp.arange(NX, dtype=jnp.float32) + 0.5) / NX
    coord_second = (jnp.arange(NY, dtype=jnp.float32) + 0.5) / NY
    coord_third = (jnp.arange(NZ, dtype=jnp.float32) + 0.5) / NZ
    pattern = jnp.zeros((NX, NY, NZ), jnp.float32)
    for term_index in range(4):
        along_first = jnp.cos(2.0 * math.pi * waves_first[term_index].astype(jnp.float32) * coord_first + phases[term_index, 0])
        along_second = jnp.cos(2.0 * math.pi * waves_second[term_index].astype(jnp.float32) * coord_second + phases[term_index, 1])
        along_third = jnp.cos(math.pi * waves_third[term_index].astype(jnp.float32) * coord_third + phases[term_index, 2])
        pattern = pattern + amplitudes[term_index] * along_first[:, None, None] * along_second[None, :, None] * along_third[None, None, :]
    return pattern


def cellwise_noise(key):
    return 0.5 * jnp.clip(jax.random.normal(key, (NX, NY, NZ), jnp.float32), -4.0, 4.0)


def draw_water_head(key, part):
    return modal_pattern(jax.random.fold_in(key, 11)) + cellwise_noise(jax.random.fold_in(key, 12))


def draw_recharge(key, part):
    return modal_pattern(jax.random.fold_in(key, 21)) + cellwise_noise(jax.random.fold_in(key, 22))


def steps_of(stream_key, extent, pieces, low, top_value):
    level, own = 1.0, jax.random.fold_in(stream_key, 6)
    for dim, shards_of in pieces:
        steps = jnp.exp(jax.random.uniform(jax.random.fold_in(own, dim), (shards_of,), jnp.float32, low / len(pieces), top_value / len(pieces)))
        level = level * jnp.repeat(steps, extent[dim] // shards_of).reshape([-1 if axis == dim else 1 for axis in range(len(extent))])
    return level


def setup_inputs(seed: int = 0) -> dict:
    keys = jax.random.split(jax.random.key(seed), 4)
    water_head = draw_water_head(jax.random.fold_in(keys[3], 71), 0)
    conductivity = jnp.clip(jnp.exp(math.log(8.0) - 2.0794415 * jax.random.uniform(keys[1], (NX, NY, NZ), jnp.float32) ** steps_of(keys[1], (NX, NY, NZ), ((0, 32), (1, 16)), -0.2, 0.2)), 1.0, 8.0)
    recharge = draw_recharge(jax.random.fold_in(keys[3], 71), 0)
    return dict(water_head=water_head, conductivity=conductivity, recharge=recharge)


def harmonic(one_side, other_side):
    return 2.0 * one_side * other_side / (one_side + other_side)

def line_solve(link_west, link_east, values):
    beneath = (-link_west).at[..., 0].set(0.0)
    overhead = (-link_east).at[..., -1].set(0.0)
    diagonal = 1.0 + link_west + link_east
    return lax.linalg.tridiagonal_solve(beneath, diagonal, overhead, values[..., None])[..., 0]

def reference(water_head, conductivity, recharge):

    def plane_delta(plane):
        below_index = jnp.maximum(plane - 1, 0).astype(jnp.int32)
        above_index = jnp.minimum(plane + 1, NZ - 1).astype(jnp.int32)
        heads_here = lax.dynamic_index_in_dim(water_head, plane, 2, keepdims=False)
        heads_below = lax.dynamic_index_in_dim(water_head, below_index, 2, keepdims=False)
        heads_above = lax.dynamic_index_in_dim(water_head, above_index, 2, keepdims=False)
        conduct_here = lax.dynamic_index_in_dim(conductivity, plane, 2, keepdims=False)
        conduct_below = lax.dynamic_index_in_dim(conductivity, below_index, 2, keepdims=False)
        conduct_above = lax.dynamic_index_in_dim(conductivity, above_index, 2, keepdims=False)
        source_here = lax.dynamic_index_in_dim(recharge, plane, 2, keepdims=False)
        heads_pad = jnp.pad(heads_here, 1)
        conduct_pad = jnp.pad(conduct_here, 1)
        heads_ew = heads_pad[:, 1:-1]
        conduct_ew = conduct_pad[:, 1:-1]
        east_face = harmonic(conduct_ew[1:-1], conduct_ew[2:])
        west_face = harmonic(conduct_ew[:-2], conduct_ew[1:-1])
        flow_east = east_face * (heads_ew[2:] - heads_ew[1:-1]) - west_face * (heads_ew[1:-1] - heads_ew[:-2])
        heads_ns = heads_pad[1:-1]
        conduct_ns = conduct_pad[1:-1]
        north_face = harmonic(conduct_ns[:, 1:-1], conduct_ns[:, 2:])
        south_face = harmonic(conduct_ns[:, :-2], conduct_ns[:, 1:-1])
        flow_north = north_face * (heads_ns[:, 2:] - heads_ns[:, 1:-1]) - south_face * (heads_ns[:, 1:-1] - heads_ns[:, :-2])
        upper_face = jnp.where(plane < NZ - 1, harmonic(conduct_here, conduct_above), 0.0)
        under_face = jnp.where(plane > 0, harmonic(conduct_below, conduct_here), 0.0)
        flow_depth = upper_face * (heads_above - heads_here) - under_face * (heads_here - heads_below)
        forcing = COEF_X * flow_east + COEF_Y * flow_north + COEF_Z * flow_depth + source_here
        first_delta = line_solve((0.5 * COEF_X * west_face).T, (0.5 * COEF_X * east_face).T, forcing.T).T
        second_delta = line_solve(0.5 * COEF_Y * south_face, 0.5 * COEF_Y * north_face, first_delta)
        return second_delta
    planes = lax.map(plane_delta, jnp.arange(NZ, dtype=jnp.int32))

    def row_result(row_index):
        second_row = lax.dynamic_index_in_dim(planes, row_index, 1, keepdims=False).T
        conduct_row = lax.dynamic_index_in_dim(conductivity, row_index, 0, keepdims=False)
        heads_row = lax.dynamic_index_in_dim(water_head, row_index, 0, keepdims=False)
        conduct_ud = jnp.pad(conduct_row, ((0, 0), (1, 1)))
        upper_face = harmonic(conduct_ud[:, 1:-1], conduct_ud[:, 2:])
        under_face = harmonic(conduct_ud[:, :-2], conduct_ud[:, 1:-1])
        third_delta = line_solve(0.5 * COEF_Z * under_face, 0.5 * COEF_Z * upper_face, second_row)
        return heads_row + third_delta
    return lax.map(row_result, jnp.arange(NX, dtype=jnp.int32))
```

```python
import functools

import jax
import jax.numpy as jnp
from jax import lax
from jax.experimental import pallas as pl
from jax.experimental.pallas import tpu as pltpu
from jax.sharding import PartitionSpec as P

COEF_Z = 8.0
COEF_X = 5120.0
COEF_Y = 5120.0

N = 32
L = 128
ROWS = N * N


def link(coef, one, other):
    return coef * (one * other) / (one + other)


def xp(i):
    return pl.ds(pl.multiple_of(i * N, N), N)


def yp(j):
    return pl.ds(j, N, stride=N)


def pack_kernel(h, k, xlo, xhi, ylo, yhi):
    for out, at in ((xlo, xp(0)), (xhi, xp(N - 1)), (ylo, yp(0)), (yhi, yp(N - 1))):
        out[0] = h[at, :]
        out[1] = k[at, :]


def factor_kernel(h, k, rc, f, bx, ex, ix, mx, by, ey, iy, my, ez, iz, wx, wy, wz, wzt):
    def y_links(j, carry):
        k0, h0, low = carry
        k1, h1 = k[yp(j), :], h[yp(j), :]
        w = link(COEF_Y, k0, k1)
        wy[xp(j), :] = w
        up = 2.0 * w * (h1 - h0)
        f[yp(j - 1), :] = up - low
        return k1, h1, up

    _, _, low = lax.fori_loop(
        1, N, y_links, (k[yp(0), :], h[yp(0), :], jnp.zeros((N, L), jnp.float32)), unroll=4
    )
    f[yp(N - 1), :] = -low

    lane = lax.broadcasted_iota(jnp.int32, (N, L), 1)

    def z_part(kk, hh):
        ku = pltpu.roll(kk, L - 1, 1)
        hu = pltpu.roll(hh, L - 1, 1)
        w = jnp.where(lane < L - 1, link(COEF_Z, kk, ku), 0.0)
        up = 2.0 * w * (hu - hh)
        return w, up - pltpu.roll(up, 1, 1)

    def x_links(i, carry):
        k0, h0, low = carry
        k1, h1 = k[xp(i), :], h[xp(i), :]
        w = link(COEF_X, k0, k1)
        wx[xp(i), :] = w
        up = 2.0 * w * (h1 - h0)
        wzi, fz = z_part(k0, h0)
        wz[xp(i - 1), :] = wzi
        f[xp(i - 1), :] = f[xp(i - 1), :] + rc[xp(i - 1), :] + fz + (up - low)
        return k1, h1, up

    k1, h1, low = lax.fori_loop(
        1, N, x_links, (k[xp(0), :], h[xp(0), :], jnp.zeros((N, L), jnp.float32)), unroll=4
    )
    wzi, fz = z_part(k1, h1)
    wz[xp(N - 1), :] = wzi
    f[xp(N - 1), :] = f[xp(N - 1), :] + rc[xp(N - 1), :] + fz - low

    for g in range(8):
        wzt[pl.ds(g, L, stride=8), :] = jnp.transpose(wz[pl.ds(g * L, L), :])

    one = jnp.ones((N, L), jnp.float32)

    def step(i, state, w, b_out, e_out, i_out):
        beta, ground, a = state
        e = w[xp(i + 1), :]
        inv = 1.0 / (beta + e + ground)
        bh = beta * inv
        eh = e * inv
        b_out[xp(i), :] = bh
        e_out[xp(i), :] = eh
        i_out[xp(i), :] = inv
        return bh * e, 1.0 + eh * ground, a + bh * ground

    def zrow(z):
        return pl.ds(pl.multiple_of(z * 8, 8), 8)

    def z_step(i, state):
        lo, hi = state
        e = wzt[zrow(i), :]
        inv = 1.0 / (lo + e)
        eh = e * inv
        ez[zrow(i), :] = eh
        iz[zrow(i), :] = inv
        lo = 1.0 + eh * lo
        t = L - 1 - i
        e = wzt[zrow(t - 1), :]
        inv = 1.0 / (hi + e)
        eh = e * inv
        ez[zrow(t), :] = eh
        iz[zrow(t), :] = inv
        hi = 1.0 + eh * hi
        return lo, hi

    def chains(i, state):
        sx, sy, sz = state
        sx = step(i, sx, wx, bx, ex, ix)
        sy = step(i, sy, wy, by, ey, iy)
        sz = z_step(2 * i - 2, sz)
        sz = z_step(2 * i - 1, sz)
        return sx, sy, sz

    zone = jnp.ones((8, L), jnp.float32)
    sx, sy, sz = lax.fori_loop(
        1,
        N - 1,
        chains,
        ((wx[xp(1), :], one, one), (wy[xp(1), :], one, one), (zone, zone)),
    )
    mx[0], mx[2], mx[1] = sx
    my[0], my[2], my[1] = sy
    for i in range(2 * N - 4, 2 * N - 1):
        sz = z_step(i, sz)
    lo, hi = sz
    mid = L // 2 - 1
    e = wzt[zrow(mid), :]
    inv = 1.0 / (hi + e)
    eh = e * inv
    ez[zrow(mid + 1), :] = eh
    iz[zrow(mid + 1), :] = inv
    iz[zrow(mid), :] = 1.0 / (lo + eh * hi)
    ez[zrow(mid), :] = jnp.zeros((8, L), jnp.float32)


def end_cell(w0, m):
    beta, a, ground = m[0], m[1], m[2]
    inv = 1.0 / (w0 + beta + a)
    wh = w0 * inv
    bh = beta * inv
    return (wh, bh, inv), (w0 * bh, wh * a, ground + bh * a)


def x_down_kernel(f_in, bx, ex, ix, mx, my, xlo, xhi, ylo, yhi, pxlo, pxhi, pylo, pyhi, out, s_out, cx, yout, f):
    south = link(COEF_Y, pylo[1], ylo[1])
    north = link(COEF_Y, yhi[1], pyhi[1])
    f[...] = f_in[...]
    f[yp(0), :] = f[yp(0), :] - 2.0 * south * (ylo[0] - pylo[0])
    f[yp(N - 1), :] = f[yp(N - 1), :] + 2.0 * north * (pyhi[0] - yhi[0])
    west = link(COEF_X, pxlo[1], xlo[1])
    east = link(COEF_X, xhi[1], pxhi[1])

    (wh, bh, inv), (mb, ma, mg) = end_cell(south, my)
    yout[0], yout[1], yout[2], yout[3], yout[4], yout[5] = wh, bh, inv, mb, ma, mg

    def step(i, state):
        s, r = state
        s_out[xp(i), :] = s * ix[xp(i), :]
        return f[xp(i + 1), :] + ex[xp(i), :] * s, r + bx[xp(i), :] * s

    s, r = lax.fori_loop(
        1, N - 1, step, (f[xp(1), :], jnp.zeros((N, L), jnp.float32)), unroll=5
    )
    s = s + 2.0 * east * (pxhi[0] - xhi[0])
    s0 = r + f[xp(0), :] - 2.0 * west * (xlo[0] - pxlo[0])
    (wh, bh, inv), (mb, ma, mg) = end_cell(west, mx)
    cx[0], cx[1], cx[2] = wh, bh, s0 * inv
    out[0], out[1], out[2], out[3], out[4] = mb, ma, mg, wh * s0, s + bh * s0


def ends_kernel(chunk, net, out):
    row = lax.broadcasted_iota(jnp.int32, (N, L), 0)

    def before(v, s):
        return jnp.where(row >= s, pltpu.roll(v, s, 0), 0.0)

    def after(v, s):
        return jnp.where(row < N - s, pltpu.roll(v, N - s, 0), 0.0)

    beta = net[0]
    ground = net[2] + after(net[1], chunk)
    rhs = net[4] + after(net[3], chunk)
    s = chunk
    while s < N:
        nxt = after(beta, s)
        inv = 1.0 / (ground + beta + nxt)
        gh, rh, bh = ground * inv, rhs * inv, beta * inv
        ground = ground + beta * before(gh, s) + nxt * after(gh, s)
        rhs = rhs + beta * before(rh, s) + nxt * after(rh, s)
        beta = beta * before(bh, s)
        s *= 2
    q = rhs / ground
    out[0] = before(q, chunk)
    out[1] = q


def x_up_kernel(ends, s_in, bx, ex, cx, by, ey, iy, ym, out, s_out, cy, d):
    last = ends[1]
    first = cx[2] + cx[0] * ends[0] + cx[1] * last
    d[xp(N - 1), :] = last
    d[xp(0), :] = first

    def back(t, nxt):
        i = N - 1 - t
        cur = (s_in[xp(i), :] + bx[xp(i), :] * first) + ex[xp(i), :] * nxt
        d[xp(i), :] = cur
        return cur

    lax.fori_loop(1, N - 1, back, last, unroll=5)

    def step(i, state):
        s, r = state
        s_out[xp(i), :] = s * iy[xp(i), :]
        return d[yp(i + 1), :] + ey[xp(i), :] * s, r + by[xp(i), :] * s

    s, r = lax.fori_loop(
        1, N - 1, step, (d[yp(1), :], jnp.zeros((N, L), jnp.float32)), unroll=5
    )
    s0 = r + d[yp(0), :]
    wh, bh, inv = ym[0], ym[1], ym[2]
    cy[...] = s0 * inv
    out[0], out[1], out[2], out[3], out[4] = ym[3], ym[4], ym[5], wh * s0, s + bh * s0


def final_kernel(ends, s_in, by, ey, ym, cy, ez, iz, h, out, d, t):
    last = ends[1]
    first = cy[...] + ym[0] * ends[0] + ym[1] * last
    d[yp(N - 1), :] = last
    d[yp(0), :] = first

    def back(u, nxt):
        j = N - 1 - u
        cur = (s_in[xp(j), :] + by[xp(j), :] * first) + ey[xp(j), :] * nxt
        d[yp(j), :] = cur
        return cur

    lax.fori_loop(1, N - 1, back, last, unroll=5)

    for g in range(8):
        t[pl.ds(g, L, stride=8), :] = jnp.transpose(d[pl.ds(g * L, L), :])

    def zrow(z):
        return pl.ds(pl.multiple_of(z * 8, 8), 8)

    mid = L // 2 - 1

    def down(i, state):
        lo, hi = state
        u = L - 1 - i
        t[zrow(i), :] = lo * iz[zrow(i), :]
        t[zrow(u), :] = hi * iz[zrow(u), :]
        return t[zrow(i + 1), :] + ez[zrow(i), :] * lo, t[zrow(u - 1), :] + ez[zrow(u), :] * hi

    lo, hi = lax.fori_loop(0, mid, down, (t[zrow(0), :], t[zrow(L - 1), :]), unroll=9)
    t[zrow(mid + 1), :] = hi * iz[zrow(mid + 1), :]
    m = (lo + ez[zrow(mid + 1), :] * hi) * iz[zrow(mid), :]
    t[zrow(mid), :] = m
    hi = t[zrow(mid + 1), :] + ez[zrow(mid + 1), :] * m
    t[zrow(mid + 1), :] = hi

    def up(i, state):
        lo, hi = state
        a = mid - i
        b = mid + 1 + i
        lo = t[zrow(a), :] + ez[zrow(a), :] * lo
        hi = t[zrow(b), :] + ez[zrow(b), :] * hi
        t[zrow(a), :] = lo
        t[zrow(b), :] = hi
        return lo, hi

    lax.fori_loop(1, mid + 1, up, (m, hi), unroll=9)
    for g in range(8):
        at = pl.ds(g * L, L)
        out[at, :] = h[at, :] + jnp.transpose(t[pl.ds(g, L, stride=8), :])


BLOCK = jax.ShapeDtypeStruct((ROWS, L), jnp.float32)


def planes(*lead):
    return jax.ShapeDtypeStruct(lead + (N, L), jnp.float32)


def call(kernel, outs, *args, scratch=(), flops=1000000):
    vmem = pl.BlockSpec(memory_space=pltpu.VMEM)
    moved = 4 * sum(a.size for a in args)
    return pl.pallas_call(
        kernel,
        out_shape=outs,
        in_specs=[vmem] * len(args),
        out_specs=jax.tree.map(lambda _: vmem, outs),
        scratch_shapes=[pltpu.VMEM(s.shape, s.dtype) for s in scratch],
        cost_estimate=pl.CostEstimate(flops=flops, bytes_accessed=moved, transcendentals=0),
    )(*args)


def neighbours(lo, hi, axis):
    count = lax.axis_size(axis)
    forward = [(i, i + 1) for i in range(count - 1)]
    backward = [(i + 1, i) for i in range(count - 1)]
    return lax.ppermute(hi, axis, forward), lax.ppermute(lo, axis, backward)


def line_ends(net, axis):
    count = lax.axis_size(axis)
    chunk = N // count
    got = lax.all_to_all(net, axis, 1, 1, tiled=True)
    ends = call(functools.partial(ends_kernel, chunk), planes(2), got, flops=100000)
    return lax.all_to_all(ends, axis, 1, 1, tiled=True)


def per_device(water_head, conductivity, recharge):
    h, k, rc = (a.reshape(ROWS, L) for a in (water_head, conductivity, recharge))
    xlo, xhi, ylo, yhi = call(pack_kernel, [planes(2)] * 4, h, k, flops=10000)
    pylo, pyhi = neighbours(ylo, yhi, "gy")
    pxlo, pxhi = neighbours(xlo, xhi, "gx")
    f, bx, ex, ix, mx, by, ey, iy, my, ez, iz = call(
        factor_kernel,
        [BLOCK] * 4 + [planes(3)] + [BLOCK] * 3 + [planes(3)] + [BLOCK] * 2,
        h,
        k,
        rc,
        scratch=[BLOCK] * 4,
        flops=20000000,
    )
    net, sx, cx, ym = call(
        x_down_kernel,
        [planes(5), BLOCK, planes(3), planes(6)],
        f, bx, ex, ix, mx, my, xlo, xhi, ylo, yhi, pxlo, pxhi, pylo, pyhi,
        scratch=[BLOCK],
    )
    ends = line_ends(net, "gx")
    net, sy, cy = call(
        x_up_kernel,
        [planes(5), BLOCK, planes()],
        ends, sx, bx, ex, cx, by, ey, iy, ym,
        scratch=[BLOCK],
    )
    ends = line_ends(net, "gy")
    out = call(
        final_kernel, BLOCK, ends, sy, by, ey, ym, cy, ez, iz, h, scratch=[BLOCK] * 2
    )
    return out.reshape(water_head.shape)


def solution(mesh):
    placed = (P("gx", "gy", None),) * 3
    return jax.shard_map(
        per_device, mesh=mesh, in_specs=placed, out_specs=P("gx", "gy", None), check_vma=False
    )
```

```python
import functools

import jax
import jax.numpy as jnp
from jax import lax
from jax.experimental import pallas as pl
from jax.experimental.pallas import tpu as pltpu
from jax.sharding import PartitionSpec as P

COEF_Z = 8.0
COEF_X = 5120.0
COEF_Y = 5120.0

N = 32
L = 128
ROWS = N * N
ROW = 8
VMEM_LIMIT = 24 << 20


def link(coef, one, other):
    return coef * (one * other) / (one + other)


def xp(i):
    return pl.ds(pl.multiple_of(i * N, N), N)


def yp(j):
    return pl.ds(j, N, stride=N)


def zp(z):
    return pl.ds(pl.multiple_of(z * 8, 8), 8)


def pack_kernel(h, k, ylo, yhi):
    for out, at in ((ylo, yp(0)), (yhi, yp(N - 1))):
        out[0] = h[at, :]
        out[1] = k[at, :]


def factor_kernel(h, k, rc, f, bx, ex, ix, mx, by, ey, iy, my, ez, iz, wx, wy, wz, wzt):
    def y_links(j, carry):
        k0, h0, low = carry
        k1, h1 = k[yp(j), :], h[yp(j), :]
        w = link(COEF_Y, k0, k1)
        wy[xp(j), :] = w
        up = 2.0 * w * (h1 - h0)
        f[yp(j - 1), :] = up - low
        return k1, h1, up

    _, _, low = lax.fori_loop(
        1, N, y_links, (k[yp(0), :], h[yp(0), :], jnp.zeros((N, L), jnp.float32)), unroll=4
    )
    f[yp(N - 1), :] = -low

    lane = lax.broadcasted_iota(jnp.int32, (N, L), 1)

    def planes_x(i, k0):
        h0 = h[xp(i), :]
        ku = pltpu.roll(k0, L - 1, 1)
        hu = pltpu.roll(h0, L - 1, 1)
        w = jnp.where(lane < L - 1, link(COEF_Z, k0, ku), 0.0)
        wz[xp(i), :] = w
        up = 2.0 * w * (hu - h0)
        f[xp(i), :] = f[xp(i), :] + rc[xp(i), :] + 2.0 * h0 + (up - pltpu.roll(up, 1, 1))
        k1 = k[xp(jnp.minimum(i + 1, N - 1)), :]
        wx[xp(i), :] = link(COEF_X, k0, k1)
        return k1

    lax.fori_loop(0, N, planes_x, k[xp(0), :], unroll=4)

    for g in range(8):
        wzt[pl.ds(g, L, stride=8), :] = jnp.transpose(wz[pl.ds(g * L, L), :])

    one = jnp.ones((N, L), jnp.float32)

    def step(i, state, e, b_out, e_out, i_out):
        beta, ground, a = state
        inv = 1.0 / (beta + e + ground)
        bh = beta * inv
        eh = e * inv
        b_out[xp(i), :] = bh
        e_out[xp(i), :] = eh
        i_out[xp(i), :] = inv
        return bh * e, 1.0 + eh * ground, a + bh * ground

    def z_step(i, state):
        lo, hi = state
        e = wzt[zp(i), :]
        inv = 1.0 / (lo + e)
        eh = e * inv
        ez[zp(i), :] = eh
        iz[zp(i), :] = inv
        lo = 1.0 + eh * lo
        t = L - 1 - i
        e = wzt[zp(t - 1), :]
        inv = 1.0 / (hi + e)
        eh = e * inv
        ez[zp(t), :] = eh
        iz[zp(t), :] = inv
        hi = 1.0 + eh * hi
        return lo, hi

    def chains(i, state):
        sx, sy, sz = state
        sx = step(i, sx, wx[xp(i), :], bx, ex, ix)
        sy = step(i, sy, wy[xp(i + 1), :], by, ey, iy)
        sz = z_step(2 * i - 2, sz)
        sz = z_step(2 * i - 1, sz)
        return sx, sy, sz

    zone = jnp.ones((8, L), jnp.float32)
    sx, sy, sz = lax.fori_loop(
        1,
        N - 1,
        chains,
        ((wx[xp(0), :], one, one), (wy[xp(1), :], one, one), (zone, zone)),
    )
    mx[0], mx[2], mx[1] = sx
    my[0], my[2], my[1] = sy
    for i in range(2 * N - 4, 2 * N - 1):
        sz = z_step(i, sz)
    lo, hi = sz
    mid = L // 2 - 1
    e = wzt[zp(mid), :]
    inv = 1.0 / (hi + e)
    eh = e * inv
    ez[zp(mid + 1), :] = eh
    iz[zp(mid + 1), :] = inv
    iz[zp(mid), :] = 1.0 / (lo + eh * hi)
    ez[zp(mid), :] = jnp.zeros((8, L), jnp.float32)


def send_segment(out, m, s0, s1, k0, k1):
    for at, value in enumerate((m[0], m[1], m[2], s0, s1, k0, k1)):
        out[pl.ds(at, N, stride=ROW), :] = value


def x_down_kernel(f_in, bx, ex, ix, mx, k, ylo, yhi, pylo, pyhi, out, s_out, f):
    south = link(COEF_Y, pylo[1], ylo[1])
    north = link(COEF_Y, yhi[1], pyhi[1])
    f[...] = f_in[...]
    f[yp(0), :] = f[yp(0), :] - 2.0 * south * (ylo[0] - pylo[0])
    f[yp(N - 1), :] = f[yp(N - 1), :] + 2.0 * north * (pyhi[0] - yhi[0])

    def step(i, state):
        s, r = state
        s_out[xp(i), :] = s * ix[xp(i), :]
        return f[xp(i + 1), :] + ex[xp(i), :] * s, r + bx[xp(i), :] * s

    s, r = lax.fori_loop(1, N - 1, step, (f[xp(1), :], f[xp(0), :]), unroll=5)
    send_segment(out, mx, r, s, k[xp(0), :], k[xp(N - 1), :])


def ends_kernel(chunk, coef, net, out):
    row = lax.broadcasted_iota(jnp.int32, (N, L), 0)

    def before(v, s):
        return jnp.where(row >= s, pltpu.roll(v, s, 0), 0.0)

    def after(v, s):
        return jnp.where(row < N - s, pltpu.roll(v, N - s, 0), 0.0)

    inner, c0, c1, s0, s1, k0, k1 = (net[pl.ds(at, N, stride=ROW), :] for at in range(7))
    w = link(coef, before(k1, chunk), k0)
    inv0 = 1.0 / (w + inner + c0)
    wh, bh = w * inv0, inner * inv0
    beta = w * bh
    ground = c1 + bh * c0 + after(wh * c0, chunk)
    rhs = s1 + bh * s0 + after(wh * s0, chunk)
    s = chunk
    while s < N:
        nxt = after(beta, s)
        inv = 1.0 / (ground + beta + nxt)
        gh, rh, lh = ground * inv, rhs * inv, beta * inv
        ground = ground + beta * before(gh, s) + nxt * after(gh, s)
        rhs = rhs + beta * before(rh, s) + nxt * after(rh, s)
        beta = beta * before(lh, s)
        s *= 2
    q = rhs / ground
    out[pl.ds(0, N, stride=2), :] = s0 * inv0 + wh * before(q, chunk) + bh * q
    out[pl.ds(1, N, stride=2), :] = q


def x_up_kernel(ends, s_in, bx, ex, h, by, ey, iy, my, ylo, yhi, out, s_out, d):
    first = ends[pl.ds(0, N, stride=2), :]
    last = ends[pl.ds(1, N, stride=2), :]
    d[xp(N - 1), :] = last - 2.0 * h[xp(N - 1), :]
    d[xp(0), :] = first - 2.0 * h[xp(0), :]

    def back(t, nxt):
        i = N - 1 - t
        cur = (s_in[xp(i), :] + bx[xp(i), :] * first) + ex[xp(i), :] * nxt
        d[xp(i), :] = cur - 2.0 * h[xp(i), :]
        return cur

    lax.fori_loop(1, N - 1, back, last, unroll=5)

    def step(i, state):
        s, r = state
        s_out[xp(i), :] = s * iy[xp(i), :]
        return d[yp(i + 1), :] + ey[xp(i), :] * s, r + by[xp(i), :] * s

    s, r = lax.fori_loop(1, N - 1, step, (d[yp(1), :], d[yp(0), :]), unroll=5)
    send_segment(out, my, r, s, ylo[1], yhi[1])


def final_kernel(ends, s_in, by, ey, ez, iz, h, out, d, t):
    first = ends[pl.ds(0, N, stride=2), :]
    last = ends[pl.ds(1, N, stride=2), :]
    d[yp(N - 1), :] = last
    d[yp(0), :] = first

    def back(u, nxt):
        j = N - 1 - u
        cur = (s_in[xp(j), :] + by[xp(j), :] * first) + ey[xp(j), :] * nxt
        d[yp(j), :] = cur
        return cur

    lax.fori_loop(1, N - 1, back, last, unroll=5)

    for g in range(8):
        t[pl.ds(g, L, stride=8), :] = jnp.transpose(d[pl.ds(g * L, L), :])

    mid = L // 2 - 1

    def down(i, state):
        lo, hi = state
        u = L - 1 - i
        t[zp(i), :] = lo * iz[zp(i), :]
        t[zp(u), :] = hi * iz[zp(u), :]
        return t[zp(i + 1), :] + ez[zp(i), :] * lo, t[zp(u - 1), :] + ez[zp(u), :] * hi

    lo, hi = lax.fori_loop(0, mid, down, (t[zp(0), :], t[zp(L - 1), :]), unroll=9)
    t[zp(mid + 1), :] = hi * iz[zp(mid + 1), :]
    m = (lo + ez[zp(mid + 1), :] * hi) * iz[zp(mid), :]
    t[zp(mid), :] = m
    hi = t[zp(mid + 1), :] + ez[zp(mid + 1), :] * m
    t[zp(mid + 1), :] = hi

    def up(i, state):
        lo, hi = state
        a = mid - i
        b = mid + 1 + i
        lo = t[zp(a), :] + ez[zp(a), :] * lo
        hi = t[zp(b), :] + ez[zp(b), :] * hi
        t[zp(a), :] = lo
        t[zp(b), :] = hi
        return lo, hi

    lax.fori_loop(1, mid + 1, up, (m, hi), unroll=9)
    for g in range(8):
        at = pl.ds(g * L, L)
        out[at, :] = h[at, :] + jnp.transpose(t[pl.ds(g, L, stride=8), :])


BLOCK = (ROWS, L)
NET = (N * ROW, L)
ENDS = (N * 2, L)


def planes(*lead):
    return lead + (N, L)


def call(kernel, outs, *args, scratch=(), in_vmem=(), out_vmem=True, flops=1000000):
    vmem = pl.BlockSpec(memory_space=pltpu.VMEM)
    moved = 4 * sum(a.size for a in args)
    args = [pltpu.with_memory_space_constraint(a, pltpu.VMEM) if i in in_vmem else a for i, a in enumerate(args)]
    make = pltpu.VMEM if out_vmem else jax.ShapeDtypeStruct
    return pl.pallas_call(
        kernel,
        out_shape=[make(s, jnp.float32) for s in outs],
        in_specs=[vmem] * len(args),
        out_specs=[vmem] * len(outs),
        scratch_shapes=[pltpu.VMEM(s, jnp.float32) for s in scratch],
        compiler_params=pltpu.CompilerParams(vmem_limit_bytes=VMEM_LIMIT),
        cost_estimate=pl.CostEstimate(flops=flops, bytes_accessed=moved, transcendentals=0),
    )(*args)


def neighbours(lo, hi, axis):
    count = lax.axis_size(axis)
    forward = [(i, i + 1) for i in range(count - 1)]
    backward = [(i + 1, i) for i in range(count - 1)]
    return lax.ppermute(hi, axis, forward), lax.ppermute(lo, axis, backward)


def line_ends(net, axis, coef):
    chunk = N // lax.axis_size(axis)
    got = lax.all_to_all(net.reshape(N, ROW, L), axis, 0, 0, tiled=True).reshape(NET)
    (ends,) = call(functools.partial(ends_kernel, chunk, coef), [ENDS], got, in_vmem=(0,), flops=100000)
    return lax.all_to_all(ends.reshape(N, 2, L), axis, 0, 0, tiled=True).reshape(ENDS)


def per_device(water_head, conductivity, recharge):
    h, k, rc = (a.reshape(ROWS, L) for a in (water_head, conductivity, recharge))
    ylo, yhi = call(pack_kernel, [planes(2)] * 2, h, k, flops=10000)
    pylo, pyhi = neighbours(ylo, yhi, "gy")
    f, bx, ex, ix, mx, by, ey, iy, my, ez, iz = call(
        factor_kernel,
        [BLOCK] * 4 + [planes(3)] + [BLOCK] * 3 + [planes(3)] + [BLOCK] * 2,
        h,
        k,
        rc,
        scratch=[BLOCK] * 4,
        flops=20000000,
    )
    net, sx = call(
        x_down_kernel,
        [NET, BLOCK],
        f, bx, ex, ix, mx, k, ylo, yhi, pylo, pyhi,
        in_vmem=(0, 1, 2, 3, 4, 6, 7, 8, 9),
        scratch=[BLOCK],
    )
    ends = line_ends(net, "gx", COEF_X)
    net, sy = call(
        x_up_kernel,
        [NET, BLOCK],
        ends, sx, bx, ex, h, by, ey, iy, my, ylo, yhi,
        in_vmem=(0, 1, 2, 3, 5, 6, 7, 8, 9, 10),
        scratch=[BLOCK],
    )
    ends = line_ends(net, "gy", COEF_Y)
    (out,) = call(
        final_kernel,
        [BLOCK],
        ends, sy, by, ey, ez, iz, h,
        in_vmem=(0, 1, 2, 3, 4, 5),
        out_vmem=False,
        scratch=[BLOCK] * 2,
    )
    return out.reshape(water_head.shape)


def solution(mesh):
    placed = (P("gx", "gy", None),) * 3
    return jax.shard_map(
        per_device, mesh=mesh, in_specs=placed, out_specs=P("gx", "gy", None), check_vma=False
    )
```

```python
import functools

import jax
import jax.numpy as jnp
from jax import lax
from jax.experimental import pallas as pl
from jax.experimental.pallas import tpu as pltpu
from jax.sharding import PartitionSpec as P

COEF_Z = 8.0
COEF_X = 5120.0
COEF_Y = 5120.0

N = 32
L = 128
ROWS = N * N
ROW = 8
VMEM_LIMIT = 24 << 20


def link(coef, one, other):
    return coef * (one * other) / (one + other)


def xp(i):
    return pl.ds(pl.multiple_of(i * N, N), N)


def yp(j):
    return pl.ds(j, N, stride=N)


def zp(z):
    return pl.ds(pl.multiple_of(z * 8, 8), 8)


def halo_planes():
    odd = lax.rem(lax.axis_index("gy"), 2)
    return (1 - odd) * (N - 1), odd * (N - 1)


def pack_kernel(h, k, far, near, sems):
    at_near, at_far = halo_planes()
    copies = [
        pltpu.make_async_copy(src.at[:, at, :], out.at[row], sems.at[2 * side + row])
        for side, (out, at) in enumerate(((far, at_far), (near, at_near)))
        for row, src in enumerate((h, k))
    ]
    for copy in copies:
        copy.start()
    for copy in copies:
        copy.wait()


def chain_step(i, state, e, b_out, e_out, i_out):
    beta, ground, a = state
    inv = 1.0 / (beta + e + ground)
    bh = beta * inv
    eh = e * inv
    b_out[xp(i), :] = bh
    e_out[xp(i), :] = eh
    i_out[xp(i), :] = inv
    return bh * e, 1.0 + eh * ground, a + bh * ground


def local_kernel(h, k, f, bx, ex, ix, mx, by, ey, iy, my, ez, iz, wx, wy, wz, wzt):
    lane = lax.broadcasted_iota(jnp.int32, (N, L), 1)
    row = lax.broadcasted_iota(jnp.int32, (N, L), 0)
    one = jnp.ones((N, L), jnp.float32)

    def flows(i, k0, kn, hn):
        h0 = h[xp(i), :]
        w = jnp.where(row < N - 1, link(COEF_Y, k0, kn), 0.0)
        wy[xp(i), :] = w
        up = 2.0 * w * (hn - h0)
        total = 2.0 * h0 + (up - pltpu.roll(up, 1, 0))
        w = jnp.where(lane < L - 1, link(COEF_Z, k0, pltpu.roll(k0, L - 1, 1)), 0.0)
        wz[xp(i), :] = w
        up = 2.0 * w * (pltpu.roll(h0, L - 1, 1) - h0)
        f[xp(i), :] = total + (up - pltpu.roll(up, 1, 1))

    def further(ref, i):
        return ref[pl.ds(pl.multiple_of(i * N, N) + 1, N), :]

    def plane(i, k0):
        k1 = k[xp(i + 1), :]
        wx[xp(i), :] = link(COEF_X, k0, k1)
        flows(i, k0, further(k, i), further(h, i))
        return k1

    k0 = k[xp(0), :]
    mx[3] = k0
    k1 = lax.fori_loop(0, N - 1, plane, k0, unroll=4)
    mx[4] = k1
    flows(N - 1, k1, pltpu.roll(k1, N - 1, 0), pltpu.roll(h[xp(N - 1), :], N - 1, 0))
    my[3], my[4] = k[yp(0), :], k[yp(N - 1), :]

    for g in range(8):
        wzt[pl.ds(g, L, stride=8), :] = jnp.transpose(wz[pl.ds(g * L, L), :])

    def z_link(i):
        return wzt[zp(i), :]

    def z_step(i, state):
        lo, hi = state
        e = z_link(i)
        inv = 1.0 / (lo + e)
        eh = e * inv
        ez[zp(i), :] = eh
        iz[zp(i), :] = inv
        lo = 1.0 + eh * lo
        t = L - 1 - i
        e = z_link(t - 1)
        inv = 1.0 / (hi + e)
        eh = e * inv
        ez[zp(t), :] = eh
        iz[zp(t), :] = inv
        hi = 1.0 + eh * hi
        return lo, hi

    def chains(i, state):
        sx, sy, sz = state
        sx = chain_step(i, sx, wx[xp(i), :], bx, ex, ix)
        sy = chain_step(i, sy, wy[yp(i), :], by, ey, iy)
        sz = z_step(2 * i - 2, sz)
        sz = z_step(2 * i - 1, sz)
        return sx, sy, sz

    zone = jnp.ones((8, L), jnp.float32)
    sx, sy, sz = lax.fori_loop(
        1, N - 1, chains, ((wx[xp(0), :], one, one), (wy[yp(0), :], one, one), (zone, zone))
    )
    mx[0], mx[2], mx[1] = sx
    my[0], my[2], my[1] = sy
    for i in range(2 * N - 4, 2 * N - 1):
        sz = z_step(i, sz)
    lo, hi = sz
    mid = L // 2 - 1
    e = z_link(mid)
    inv = 1.0 / (hi + e)
    eh = e * inv
    ez[zp(mid + 1), :] = eh
    iz[zp(mid + 1), :] = inv
    iz[zp(mid), :] = 1.0 / (lo + eh * hi)
    ez[zp(mid), :] = jnp.zeros((8, L), jnp.float32)


def send_segment(out, m, s0, s1):
    for at, value in enumerate((m[0], m[1], m[2], s0, s1, m[3], m[4])):
        out[pl.ds(at, N, stride=ROW), :] = value


def x_down_kernel(f, rc, bx, ex, ix, mx, far, near, far_in, near_in, out, s_out, g):
    g[...] = f[...] + rc[...]
    at_near, at_far = halo_planes()
    for at, mine, theirs in ((at_far, far, far_in), (at_near, near, near_in)):
        w = link(COEF_Y, mine[1], theirs[1])
        g[yp(at), :] = g[yp(at), :] + 2.0 * w * (theirs[0] - mine[0])

    def step(i, state):
        s, r = state
        s_out[xp(i), :] = s * ix[xp(i), :]
        return g[xp(i + 1), :] + ex[xp(i), :] * s, r + bx[xp(i), :] * s

    s, r = lax.fori_loop(
        1, N - 1, step, (g[xp(1), :], g[xp(0), :]), unroll=5
    )
    send_segment(out, mx, r, s)


def ends_kernel(chunk, coef, net, out):
    row = lax.broadcasted_iota(jnp.int32, (N, L), 0)

    def before(v, s):
        return jnp.where(row >= s, pltpu.roll(v, s, 0), 0.0)

    def after(v, s):
        return jnp.where(row < N - s, pltpu.roll(v, N - s, 0), 0.0)

    inner, c0, c1, s0, s1, k0, k1 = (net[pl.ds(at, N, stride=ROW), :] for at in range(7))
    w = link(coef, before(k1, chunk), k0)
    inv0 = 1.0 / (w + inner + c0)
    wh, bh = w * inv0, inner * inv0
    beta = w * bh
    ground = c1 + bh * c0 + after(wh * c0, chunk)
    rhs = s1 + bh * s0 + after(wh * s0, chunk)
    s = chunk
    while s < N:
        nxt = after(beta, s)
        inv = 1.0 / (ground + beta + nxt)
        gh, rh, lh = ground * inv, rhs * inv, beta * inv
        ground = ground + beta * before(gh, s) + nxt * after(gh, s)
        rhs = rhs + beta * before(rh, s) + nxt * after(rh, s)
        beta = beta * before(lh, s)
        s *= 2
    q = rhs / ground
    out[pl.ds(0, N, stride=2), :] = s0 * inv0 + wh * before(q, chunk) + bh * q
    out[pl.ds(1, N, stride=2), :] = q


def x_up_kernel(ends, s_in, bx, ex, h, by, ey, iy, my, out, s_out, d):
    first = ends[pl.ds(0, N, stride=2), :]
    last = ends[pl.ds(1, N, stride=2), :]
    d[xp(N - 1), :] = last - 2.0 * h[xp(N - 1), :]
    d[xp(0), :] = first - 2.0 * h[xp(0), :]

    def back(t, nxt):
        i = N - 1 - t
        cur = (s_in[xp(i), :] + bx[xp(i), :] * first) + ex[xp(i), :] * nxt
        d[xp(i), :] = cur - 2.0 * h[xp(i), :]
        return cur

    lax.fori_loop(1, N - 1, back, last, unroll=5)

    def step(i, state):
        s, r = state
        s_out[xp(i), :] = s * iy[xp(i), :]
        return d[yp(i + 1), :] + ey[xp(i), :] * s, r + by[xp(i), :] * s

    s, r = lax.fori_loop(1, N - 1, step, (d[yp(1), :], d[yp(0), :]), unroll=5)
    send_segment(out, my, r, s)


def final_kernel(ends, s_in, by, ey, ez, iz, h, out, d, t, sems):
    first = ends[pl.ds(0, N, stride=2), :]
    last = ends[pl.ds(1, N, stride=2), :]
    d[xp(N - 1), :] = last
    d[xp(0), :] = first

    def back(u, nxt):
        j = N - 1 - u
        cur = (s_in[xp(j), :] + by[xp(j), :] * first) + ey[xp(j), :] * nxt
        d[xp(j), :] = cur
        return cur

    lax.fori_loop(1, N - 1, back, last, unroll=5)

    for g in range(8):
        lines = jnp.concatenate([d[yp(i), :] for i in range(4 * g, 4 * g + 4)])
        t[pl.ds(g, L, stride=8), :] = jnp.transpose(lines)

    mid = L // 2 - 1

    def down(i, state):
        lo, hi = state
        u = L - 1 - i
        t[zp(i), :] = lo * iz[zp(i), :]
        t[zp(u), :] = hi * iz[zp(u), :]
        return t[zp(i + 1), :] + ez[zp(i), :] * lo, t[zp(u - 1), :] + ez[zp(u), :] * hi

    lo, hi = lax.fori_loop(0, mid, down, (t[zp(0), :], t[zp(L - 1), :]), unroll=9)
    t[zp(mid + 1), :] = hi * iz[zp(mid + 1), :]
    m = (lo + ez[zp(mid + 1), :] * hi) * iz[zp(mid), :]
    t[zp(mid), :] = m
    hi = t[zp(mid + 1), :] + ez[zp(mid + 1), :] * m
    t[zp(mid + 1), :] = hi

    def up(i, state):
        lo, hi = state
        a = mid - i
        b = mid + 1 + i
        lo = t[zp(a), :] + ez[zp(a), :] * lo
        hi = t[zp(b), :] + ez[zp(b), :] * hi
        t[zp(a), :] = lo
        t[zp(b), :] = hi
        return lo, hi

    lax.fori_loop(1, mid + 1, up, (m, hi), unroll=9)
    copies = []
    for g in range(8):
        at = pl.ds(g * L, L)
        d[at, :] = h[at, :] + jnp.transpose(t[pl.ds(g, L, stride=8), :])
        copies.append(pltpu.make_async_copy(d.at[at, :], out.at[at, :], sems.at[g]))
        copies[g].start()
    for copy in copies:
        copy.wait()


BLOCK = (ROWS, L)
NET = (N * ROW, L)
ENDS = (N * 2, L)


def planes(*lead):
    return lead + (N, L)


def call(kernel, outs, *args, scratch=(), sems=0, hbm_in=(), hbm_out=False, flops=1000000):
    spec = {True: pl.BlockSpec(memory_space=pltpu.HBM), False: pl.BlockSpec(memory_space=pltpu.VMEM)}
    moved = 4 * sum(a.size for a in args)
    args = [
        pltpu.with_memory_space_constraint(a, pltpu.HBM if i in hbm_in else pltpu.VMEM)
        for i, a in enumerate(args)
    ]
    make = jax.ShapeDtypeStruct if hbm_out else pltpu.VMEM
    scratch_shapes = [pltpu.VMEM(s, jnp.float32) for s in scratch]
    if sems:
        scratch_shapes.append(pltpu.SemaphoreType.DMA((sems,)))
    return pl.pallas_call(
        kernel,
        out_shape=[make(s, jnp.float32) for s in outs],
        in_specs=[spec[i in hbm_in] for i in range(len(args))],
        out_specs=[spec[hbm_out]] * len(outs),
        scratch_shapes=scratch_shapes,
        compiler_params=pltpu.CompilerParams(vmem_limit_bytes=VMEM_LIMIT),
        cost_estimate=pl.CostEstimate(flops=flops, bytes_accessed=moved, transcendentals=0),
    )(*args)


def line_ends(net, axis, coef):
    chunk = N // lax.axis_size(axis)
    got = lax.all_to_all(net.reshape(N, ROW, L), axis, 0, 0, tiled=True).reshape(NET)
    (ends,) = call(functools.partial(ends_kernel, chunk, coef), [ENDS], got, flops=100000)
    return lax.all_to_all(ends.reshape(N, 2, L), axis, 0, 0, tiled=True).reshape(ENDS)


def per_device(water_head, conductivity, recharge):
    h, k, rc = (a.reshape(ROWS, L) for a in (water_head, conductivity, recharge))
    far, near = call(
        pack_kernel, [planes(2)] * 2, water_head, conductivity, sems=4, hbm_in=(0, 1), flops=10000
    )
    count = lax.axis_size("gy")
    across = [(i, i + 1) for i in range(1, count - 1, 2)]
    far_in = lax.ppermute(far, "gy", across + [(i, j) for j, i in across])
    near_in = lax.ppermute(near, "gy", [(i, i ^ 1) for i in range(count)])
    f, bx, ex, ix, mx, by, ey, iy, my, ez, iz = call(
        local_kernel,
        [BLOCK] * 4 + [planes(5)] + [BLOCK] * 3 + [planes(5)] + [BLOCK] * 2,
        h, k,
        scratch=[BLOCK] * 4,
        flops=20000000,
    )
    net, sx = call(
        x_down_kernel,
        [NET, BLOCK],
        f, rc, bx, ex, ix, mx, far, near, far_in, near_in,
        scratch=[BLOCK],
    )
    ends = line_ends(net, "gx", COEF_X)
    net, sy = call(x_up_kernel, [NET, BLOCK], ends, sx, bx, ex, h, by, ey, iy, my, scratch=[BLOCK])
    ends = line_ends(net, "gy", COEF_Y)
    (out,) = call(
        final_kernel, [BLOCK], ends, sy, by, ey, ez, iz, h, hbm_out=True, scratch=[BLOCK] * 2, sems=8
    )
    return out.reshape(water_head.shape)


def solution(mesh):
    placed = (P("gx", "gy", None),) * 3
    return jax.shard_map(
        per_device, mesh=mesh, in_specs=placed, out_specs=P("gx", "gy", None), check_vma=False
    )
```

```python
import functools

import jax
import jax.numpy as jnp
from jax import lax
from jax.experimental import pallas as pl
from jax.experimental.pallas import tpu as pltpu
from jax.sharding import PartitionSpec as P

COEF_Z = 8.0
COEF_X = 5120.0
COEF_Y = 5120.0

N = 32
L = 128
ROWS = N * N
ROW = 8
LAST = L // 2 - 1
MID = LAST // 2
VMEM_LIMIT = 24 << 20


def link(coef, one, other):
    return coef * (one * other) / (one + other)


def xp(i):
    return pl.ds(pl.multiple_of(i * N, N), N)


def yp(j):
    return pl.ds(j, N, stride=N)


def zp(z):
    return pl.ds(pl.multiple_of(z * 8, 8), 8)


def halo_planes():
    odd = lax.rem(lax.axis_index("gy"), 2)
    return (1 - odd) * (N - 1), odd * (N - 1)


def pack_kernel(h, k, far, near, sems):
    at_near, at_far = halo_planes()
    copies = [
        pltpu.make_async_copy(src.at[:, at, :], out.at[row], sems.at[2 * side + row])
        for side, (out, at) in enumerate(((far, at_far), (near, at_near)))
        for row, src in enumerate((h, k))
    ]
    for copy in copies:
        copy.start()
    for copy in copies:
        copy.wait()


def chain_step(i, state, e, b_out, e_out, i_out):
    beta, ground, a = state
    inv = 1.0 / (beta + e + ground)
    bh = beta * inv
    eh = e * inv
    b_out[xp(i), :] = bh
    e_out[xp(i), :] = eh
    i_out[xp(i), :] = inv
    return bh * e, 1.0 + eh * ground, a + bh * ground


def local_kernel(h, k, f, bx, ex, ix, mx, by, ey, iy, my, zb, ze, zi, ez, iz, wx, wy, wz, wzt):
    lane = lax.broadcasted_iota(jnp.int32, (N, L), 1)
    row = lax.broadcasted_iota(jnp.int32, (N, L), 0)
    one = jnp.ones((N, L), jnp.float32)
    coef_y = jnp.where(row < N - 1, COEF_Y, 0.0)
    coef_z = jnp.where(lane < L - 1, COEF_Z, 0.0)

    def flows(i, k0, kn, hn):
        h0 = 2.0 * h[xp(i), :]
        w = link(coef_y, k0, kn)
        wy[xp(i), :] = w
        up = w * (2.0 * hn - h0)
        total = h0 + (up - pltpu.roll(up, 1, 0))
        w = link(coef_z, k0, pltpu.roll(k0, L - 1, 1))
        wz[xp(i), :] = w
        up = w * (pltpu.roll(h0, L - 1, 1) - h0)
        f[xp(i), :] = total + (up - pltpu.roll(up, 1, 1))

    def further(ref, i):
        return ref[pl.ds(pl.multiple_of(i * N, N) + 1, N), :]

    def plane(i, k0):
        k1 = k[xp(i + 1), :]
        wx[xp(i), :] = link(COEF_X, k0, k1)
        flows(i, k0, further(k, i), further(h, i))
        return k1

    k0 = k[xp(0), :]
    mx[3] = k0
    k1 = lax.fori_loop(1, N - 1, plane, plane(0, k0), unroll=5)
    mx[4] = k1
    flows(N - 1, k1, pltpu.roll(k1, N - 1, 0), pltpu.roll(h[xp(N - 1), :], N - 1, 0))
    my[3], my[4] = k[yp(0), :], k[yp(N - 1), :]

    for g in range(8):
        wzt[pl.ds(g, L, stride=8), :] = jnp.transpose(wz[pl.ds(g * L, L), :])

    def odd_cell(m):
        w0 = wzt[zp(2 * m), :]
        w1 = wzt[zp(2 * m + 1), :]
        inv = 1.0 / (1.0 + w0 + w1)
        b = w0 * inv
        e = w1 * inv
        zb[zp(m), :] = b
        ze[zp(m), :] = e
        zi[zp(m), :] = inv
        return b, e, b * w1

    def even_cell(m, ground, past):
        inv = 1.0 / (ground + past)
        eh = past * inv
        ez[zp(m), :] = eh
        iz[zp(m), :] = inv
        return eh * ground

    def z_step(q, state):
        lo, (b0, e0, w0), o1, hi, p0, p1 = state
        lo = (1.0 + e0 + o1[0]) + even_cell(q, lo, w0)
        hi = (1.0 + p0[0] + p1[1]) + even_cell(LAST - q, hi, p0[2])
        return lo, o1, odd_cell(q + 2), hi, p1, odd_cell(LAST - 3 - q)

    def chains(i, state):
        sx, sy, sz = state
        sx = chain_step(i, sx, wx[xp(i), :], bx, ex, ix)
        sy = chain_step(i, sy, wy[yp(i), :], by, ey, iy)
        return sx, sy, z_step(i - 1, sz)

    o0, o1 = odd_cell(0), odd_cell(1)
    top, p0, p1 = odd_cell(LAST), odd_cell(LAST - 1), odd_cell(LAST - 2)
    sz = (1.0 + o0[0], o0, o1, 1.0 + top[0] + p0[1], p0, p1)
    sx, sy, sz = lax.fori_loop(
        1, N - 1, chains, ((wx[xp(0), :], one, one), (wy[yp(0), :], one, one), sz), unroll=3
    )
    mx[0], mx[2], mx[1] = sx
    my[0], my[2], my[1] = sy
    lo, (b0, e0, w0), o1, hi, p0, p1 = sz
    lo = (1.0 + e0 + o1[0]) + even_cell(MID - 1, lo, w0)
    hi = (1.0 + p0[0] + p1[1]) + even_cell(MID + 2, hi, p0[2])
    lo = lo + even_cell(MID + 1, hi, p1[2])
    iz[zp(MID), :] = 1.0 / lo


def send_segment(out, m, s0, s1):
    for at, value in enumerate((m[0], m[1], m[2], s0, s1, m[3], m[4])):
        out[pl.ds(at, N, stride=ROW), :] = value


def x_down_kernel(f, rc, bx, ex, ix, mx, far, near, far_in, near_in, out, s_out, g):
    g[...] = f[...] + rc[...]
    at_near, at_far = halo_planes()
    for at, mine, theirs in ((at_far, far, far_in), (at_near, near, near_in)):
        w = link(COEF_Y, mine[1], theirs[1])
        g[yp(at), :] = g[yp(at), :] + 2.0 * w * (theirs[0] - mine[0])

    def step(i, state):
        s, r = state
        s_out[xp(i), :] = s * ix[xp(i), :]
        return g[xp(i + 1), :] + ex[xp(i), :] * s, r + bx[xp(i), :] * s

    s, r = lax.fori_loop(
        1, N - 1, step, (g[xp(1), :], g[xp(0), :]), unroll=5
    )
    send_segment(out, mx, r, s)


def ends_kernel(chunk, coef, net, out):
    row = lax.broadcasted_iota(jnp.int32, (N, L), 0)

    def before(v, s):
        return jnp.where(row >= s, pltpu.roll(v, s, 0), 0.0)

    def after(v, s):
        return jnp.where(row < N - s, pltpu.roll(v, N - s, 0), 0.0)

    inner, c0, c1, s0, s1, k0, k1 = (net[pl.ds(at, N, stride=ROW), :] for at in range(7))
    w = link(coef, before(k1, chunk), k0)
    inv0 = 1.0 / (w + inner + c0)
    wh, bh = w * inv0, inner * inv0
    beta = w * bh
    ground = c1 + bh * c0 + after(wh * c0, chunk)
    rhs = s1 + bh * s0 + after(wh * s0, chunk)
    s = chunk
    while s < N:
        nxt = after(beta, s)
        inv = 1.0 / (ground + beta + nxt)
        gh, rh, lh = ground * inv, rhs * inv, beta * inv
        ground = ground + beta * before(gh, s) + nxt * after(gh, s)
        rhs = rhs + beta * before(rh, s) + nxt * after(rh, s)
        beta = beta * before(lh, s)
        s *= 2
    q = rhs / ground
    out[pl.ds(0, N, stride=2), :] = s0 * inv0 + wh * before(q, chunk) + bh * q
    out[pl.ds(1, N, stride=2), :] = q


def x_up_kernel(ends, s_in, bx, ex, h, by, ey, iy, my, out, s_out, d):
    first = ends[pl.ds(0, N, stride=2), :]
    last = ends[pl.ds(1, N, stride=2), :]
    d[xp(N - 1), :] = last - 2.0 * h[xp(N - 1), :]
    d[xp(0), :] = first - 2.0 * h[xp(0), :]

    def back(t, nxt):
        i = N - 1 - t
        cur = (s_in[xp(i), :] + bx[xp(i), :] * first) + ex[xp(i), :] * nxt
        d[xp(i), :] = cur - 2.0 * h[xp(i), :]
        return cur

    lax.fori_loop(1, N - 1, back, last, unroll=10)

    def step(i, state):
        s, r = state
        s_out[xp(i), :] = s * iy[xp(i), :]
        return d[yp(i + 1), :] + ey[xp(i), :] * s, r + by[xp(i), :] * s

    s, r = lax.fori_loop(1, N - 1, step, (d[yp(1), :], d[yp(0), :]), unroll=10)
    send_segment(out, my, r, s)


def final_kernel(ends, s_in, by, ey, zb, ze, zi, ez, iz, h, out, d, t, sems):
    first = ends[pl.ds(0, N, stride=2), :]
    last = ends[pl.ds(1, N, stride=2), :]
    d[xp(N - 1), :] = last
    d[xp(0), :] = first

    def back(u, nxt):
        j = N - 1 - u
        cur = (s_in[xp(j), :] + by[xp(j), :] * first) + ey[xp(j), :] * nxt
        d[xp(j), :] = cur
        return cur

    lax.fori_loop(1, N - 1, back, last, unroll=10)

    for g in range(8):
        lines = jnp.concatenate([d[yp(i), :] for i in range(4 * g, 4 * g + 4)])
        t[pl.ds(g, L, stride=8), :] = jnp.transpose(lines)

    def reduced(m):
        return (t[zp(2 * m), :] + zb[zp(m), :] * t[zp(2 * m + 1), :]) + ze[zp(m - 1), :] * t[zp(2 * m - 1), :]

    def down(q, state):
        lo, hi = state
        m = LAST - q
        next_lo = reduced(q + 1) + ez[zp(q), :] * lo
        next_hi = reduced(m - 1) + ez[zp(m), :] * hi
        t[zp(2 * q), :] = lo * iz[zp(q), :]
        t[zp(2 * m), :] = hi * iz[zp(m), :]
        return next_lo, next_hi

    lo, hi = t[zp(0), :] + zb[zp(0), :] * t[zp(1), :], reduced(LAST)
    lo, hi = lax.fori_loop(0, MID, down, (lo, hi), unroll=31)
    mid = (lo + ez[zp(MID + 1), :] * hi) * iz[zp(MID), :]
    t[zp(2 * MID), :] = mid
    t[zp(2 * MID + 2), :] = hi * iz[zp(MID + 1), :]

    def odd_back(m, below, above):
        at = zp(2 * m + 1)
        t[at, :] = (zi[zp(m), :] * t[at, :] + zb[zp(m), :] * below) + ze[zp(m), :] * above

    def up(q, state):
        lo, hi = state
        a = MID - 1 - q
        b = MID + 1 + q
        next_lo = t[zp(2 * a), :] + ez[zp(a), :] * lo
        next_hi = t[zp(2 * b), :] + ez[zp(b), :] * hi
        t[zp(2 * a), :] = next_lo
        t[zp(2 * b), :] = next_hi
        odd_back(a, next_lo, lo)
        odd_back(b - 1, hi, next_hi)
        return next_lo, next_hi

    lo, hi = lax.fori_loop(0, MID, up, (mid, mid), unroll=31)
    next_hi = t[zp(2 * LAST), :] + ez[zp(LAST), :] * hi
    t[zp(2 * LAST), :] = next_hi
    odd_back(LAST - 1, hi, next_hi)
    odd_back(LAST, next_hi, 0.0)

    copies = []
    for g in range(8):
        at = pl.ds(g * L, L)
        d[at, :] = h[at, :] + jnp.transpose(t[pl.ds(g, L, stride=8), :])
        copies.append(pltpu.make_async_copy(d.at[at, :], out.at[at, :], sems.at[g]))
        copies[g].start()
    for copy in copies:
        copy.wait()


BLOCK = (ROWS, L)
HALF = (ROWS // 2, L)
NET = (N * ROW, L)
ENDS = (N * 2, L)


def planes(*lead):
    return lead + (N, L)


def call(kernel, outs, *args, scratch=(), sems=0, hbm_in=(), hbm_out=False, flops=1000000):
    spec = {True: pl.BlockSpec(memory_space=pltpu.HBM), False: pl.BlockSpec(memory_space=pltpu.VMEM)}
    moved = 4 * sum(a.size for a in args)
    args = [
        pltpu.with_memory_space_constraint(a, pltpu.HBM if i in hbm_in else pltpu.VMEM)
        for i, a in enumerate(args)
    ]
    make = jax.ShapeDtypeStruct if hbm_out else pltpu.VMEM
    scratch_shapes = [pltpu.VMEM(s, jnp.float32) for s in scratch]
    if sems:
        scratch_shapes.append(pltpu.SemaphoreType.DMA((sems,)))
    return pl.pallas_call(
        kernel,
        out_shape=[make(s, jnp.float32) for s in outs],
        in_specs=[spec[i in hbm_in] for i in range(len(args))],
        out_specs=[spec[hbm_out]] * len(outs),
        scratch_shapes=scratch_shapes,
        compiler_params=pltpu.CompilerParams(vmem_limit_bytes=VMEM_LIMIT),
        cost_estimate=pl.CostEstimate(flops=flops, bytes_accessed=moved, transcendentals=0),
    )(*args)


def line_ends(net, axis, coef):
    chunk = N // lax.axis_size(axis)
    got = lax.all_to_all(net.reshape(N, ROW, L), axis, 0, 0, tiled=True).reshape(NET)
    (ends,) = call(functools.partial(ends_kernel, chunk, coef), [ENDS], got, flops=100000)
    return lax.all_to_all(ends.reshape(N, 2, L), axis, 0, 0, tiled=True).reshape(ENDS)


def per_device(water_head, conductivity, recharge):
    h, k, rc = (a.reshape(ROWS, L) for a in (water_head, conductivity, recharge))
    far, near = call(
        pack_kernel, [planes(2)] * 2, water_head, conductivity, sems=4, hbm_in=(0, 1), flops=10000
    )
    count = lax.axis_size("gy")
    across = [(i, i + 1) for i in range(1, count - 1, 2)]
    far_in = lax.ppermute(far, "gy", across + [(i, j) for j, i in across])
    near_in = lax.ppermute(near, "gy", [(i, i ^ 1) for i in range(count)])
    f, bx, ex, ix, mx, by, ey, iy, my, *z = call(
        local_kernel,
        [BLOCK] * 4 + [planes(5)] + [BLOCK] * 3 + [planes(5)] + [HALF] * 5,
        h, k,
        scratch=[BLOCK] * 4,
        flops=20000000,
    )
    net, sx = call(
        x_down_kernel,
        [NET, BLOCK],
        f, rc, bx, ex, ix, mx, far, near, far_in, near_in,
        scratch=[BLOCK],
    )
    ends = line_ends(net, "gx", COEF_X)
    net, sy = call(x_up_kernel, [NET, BLOCK], ends, sx, bx, ex, h, by, ey, iy, my, scratch=[BLOCK])
    ends = line_ends(net, "gy", COEF_Y)
    (out,) = call(
        final_kernel, [BLOCK], ends, sy, by, ey, *z, h, hbm_out=True, scratch=[BLOCK] * 2, sems=8
    )
    return out.reshape(water_head.shape)


def solution(mesh):
    placed = (P("gx", "gy", None),) * 3
    return jax.shard_map(
        per_device, mesh=mesh, in_specs=placed, out_specs=P("gx", "gy", None), check_vma=False
    )
```

```python
import functools

import jax
import jax.numpy as jnp
from jax import lax
from jax.experimental import pallas as pl
from jax.experimental.pallas import tpu as pltpu
from jax.sharding import PartitionSpec as P

COEF_Z = 8.0
COEF_X = 5120.0
COEF_Y = 5120.0

N = 32
L = 128
ROWS = N * N
ROW = 5
LAST = L // 2 - 1
MID = LAST // 2
VMEM_LIMIT = 24 << 20


def link(coef, one, other):
    return coef * (one * other) / (one + other)


def xp(i):
    return pl.ds(pl.multiple_of(i * N, N), N)


def yp(j):
    return pl.ds(j, N, stride=N)


def zp(z):
    return pl.ds(pl.multiple_of(z * 8, 8), 8)


def halo_planes():
    odd = lax.rem(lax.axis_index("gy"), 2)
    return (1 - odd) * (N - 1), odd * (N - 1)


def pack_kernel(h, k, far, near, sems):
    at_near, at_far = halo_planes()
    copies = [
        pltpu.make_async_copy(src.at[:, at, :], out.at[row], sems.at[2 * side + row])
        for side, (out, at) in enumerate(((far, at_far), (near, at_near)))
        for row, src in enumerate((h, k))
    ]
    for copy in copies:
        copy.start()
    for copy in copies:
        copy.wait()


def chain_step(i, state, e, b_out, e_out, i_out):
    beta, ground, a = state
    inv = 1.0 / (beta + e + ground)
    bh = beta * inv
    eh = e * inv
    b_out[xp(i), :] = bh
    e_out[xp(i), :] = eh
    i_out[xp(i), :] = inv
    return bh * e, 1.0 + eh * ground, a + bh * ground


def local_kernel(h, k, f, bx, ex, ix, mx, by, ey, iy, my, zb, ze, zi, ez, iz, wx, wy, wz, wzt):
    lane = lax.broadcasted_iota(jnp.int32, (N, L), 1)
    row = lax.broadcasted_iota(jnp.int32, (N, L), 0)
    one = jnp.ones((N, L), jnp.float32)
    coef_y = jnp.where(row < N - 1, COEF_Y, 0.0)
    coef_z = jnp.where(lane < L - 1, COEF_Z, 0.0)

    def flows(i, k0, kn, hn):
        h0 = 2.0 * h[xp(i), :]
        w = link(coef_y, k0, kn)
        wy[xp(i), :] = w
        up = w * (2.0 * hn - h0)
        total = h0 + (up - pltpu.roll(up, 1, 0))
        w = link(coef_z, k0, pltpu.roll(k0, L - 1, 1))
        wz[xp(i), :] = w
        up = w * (pltpu.roll(h0, L - 1, 1) - h0)
        f[xp(i), :] = total + (up - pltpu.roll(up, 1, 1))

    def further(ref, i):
        return ref[pl.ds(pl.multiple_of(i * N, N) + 1, N), :]

    def plane(i, k0):
        k1 = k[xp(i + 1), :]
        wx[xp(i), :] = link(COEF_X, k0, k1)
        flows(i, k0, further(k, i), further(h, i))
        return k1

    k0 = k[xp(0), :]
    k1 = lax.fori_loop(1, N - 1, plane, plane(0, k0), unroll=5)
    flows(N - 1, k1, pltpu.roll(k1, N - 1, 0), pltpu.roll(h[xp(N - 1), :], N - 1, 0))

    for g in range(8):
        wzt[pl.ds(g, L, stride=8), :] = jnp.transpose(wz[pl.ds(g * L, L), :])

    def odd_cell(m):
        w0 = wzt[zp(2 * m), :]
        w1 = wzt[zp(2 * m + 1), :]
        inv = 1.0 / (1.0 + w0 + w1)
        b = w0 * inv
        e = w1 * inv
        zb[zp(m), :] = b
        ze[zp(m), :] = e
        zi[zp(m), :] = inv
        return b, e, b * w1

    def even_cell(m, ground, past):
        inv = 1.0 / (ground + past)
        eh = past * inv
        ez[zp(m), :] = eh
        iz[zp(m), :] = inv
        return eh * ground

    def z_step(q, state):
        lo, (b0, e0, w0), o1, hi, p0, p1 = state
        lo = (1.0 + e0 + o1[0]) + even_cell(q, lo, w0)
        hi = (1.0 + p0[0] + p1[1]) + even_cell(LAST - q, hi, p0[2])
        return lo, o1, odd_cell(q + 2), hi, p1, odd_cell(LAST - 3 - q)

    def chains(i, state):
        sx, sy, sz = state
        sx = chain_step(i, sx, wx[xp(i), :], bx, ex, ix)
        sy = chain_step(i, sy, wy[yp(i), :], by, ey, iy)
        return sx, sy, z_step(i - 1, sz)

    o0, o1 = odd_cell(0), odd_cell(1)
    top, p0, p1 = odd_cell(LAST), odd_cell(LAST - 1), odd_cell(LAST - 2)
    sz = (1.0 + o0[0], o0, o1, 1.0 + top[0] + p0[1], p0, p1)
    sx, sy, sz = lax.fori_loop(
        1, N - 1, chains, ((wx[xp(0), :], one, one), (wy[yp(0), :], one, one), sz), unroll=3
    )
    close_segment(mx, sx, COEF_X * k[xp(0), :], COEF_X * k[xp(N - 1), :])
    close_segment(my, sy, COEF_Y * k[yp(0), :], COEF_Y * k[yp(N - 1), :])
    lo, (b0, e0, w0), o1, hi, p0, p1 = sz
    lo = (1.0 + e0 + o1[0]) + even_cell(MID - 1, lo, w0)
    hi = (1.0 + p0[0] + p1[1]) + even_cell(MID + 2, hi, p0[2])
    lo = lo + even_cell(MID + 1, hi, p1[2])
    iz[zp(MID), :] = 1.0 / lo


def close_segment(m, state, half0, half1):
    beta, c, a = state
    inv0 = 1.0 / (half0 + beta + a)
    wh, bh = half0 * inv0, beta * inv0
    past = wh * beta
    c = c + bh * a
    inv1 = 1.0 / (past + half1 + c)
    lh, uh = past * inv1, half1 * inv1
    for at, value in enumerate((lh * half1, wh * a + lh * c, uh * c, wh, bh, inv0, lh, uh, inv1)):
        m[at] = value


def send_segment(out, shares, m, r, s):
    s = s + m[4] * r
    for at, value in enumerate((m[0], m[1], m[2], m[3] * r + m[6] * s, m[7] * s)):
        out[pl.ds(at, N, stride=ROW), :] = value
    shares[0], shares[1] = m[5] * r, m[8] * s


def end_cells(ends, shares, m):
    before, after = ends[pl.ds(0, N, stride=2), :], ends[pl.ds(1, N, stride=2), :]
    last = shares[1] + m[6] * before + m[7] * after
    return shares[0] + m[3] * before + m[4] * last, last


def x_down_kernel(f, rc, bx, ex, ix, mx, far, near, far_in, near_in, out, s_out, shares, g):
    g[...] = f[...] + rc[...]
    at_near, at_far = halo_planes()
    for at, mine, theirs in ((at_far, far, far_in), (at_near, near, near_in)):
        w = link(COEF_Y, mine[1], theirs[1])
        g[yp(at), :] = g[yp(at), :] + 2.0 * w * (theirs[0] - mine[0])

    def step(i, state):
        s, r = state
        s_out[xp(i), :] = s * ix[xp(i), :]
        return g[xp(i + 1), :] + ex[xp(i), :] * s, r + bx[xp(i), :] * s

    s, r = lax.fori_loop(
        1, N - 1, step, (g[xp(1), :], g[xp(0), :]), unroll=5
    )
    send_segment(out, shares, mx, r, s)


def ends_kernel(chunk, net, out):
    row = lax.broadcasted_iota(jnp.int32, (N, L), 0)

    def before(v, s):
        return jnp.where(row >= s, pltpu.roll(v, s, 0), 0.0)

    def after(v, s):
        return jnp.where(row < N - s, pltpu.roll(v, N - s, 0), 0.0)

    past, g0, g1, r0, r1 = (net[pl.ds(at, N, stride=ROW), :] for at in range(ROW))
    final = row >= N - chunk
    inv_final = 1.0 / (past + g1)
    share = jnp.where(final, past * inv_final, 0.0)
    beta = before(past, chunk)
    ground = g0 + before(g1, chunk) + share * g1
    rhs = r0 + before(r1, chunk) + share * r1
    s = chunk
    while s < N:
        nxt = after(beta, s)
        inv = 1.0 / (ground + beta + nxt)
        gh, rh, lh = ground * inv, rhs * inv, beta * inv
        ground = ground + beta * before(gh, s) + nxt * after(gh, s)
        rhs = rhs + beta * before(rh, s) + nxt * after(rh, s)
        beta = beta * before(lh, s)
        s *= 2
    q = rhs / ground
    out[pl.ds(0, N, stride=2), :] = q
    out[pl.ds(1, N, stride=2), :] = jnp.where(final, (r1 + past * q) * inv_final, after(q, chunk))


def x_up_kernel(ends, s_in, bx, ex, mx, shares, h, by, ey, iy, my, out, s_out, shares_y, d):
    first, last = end_cells(ends, shares, mx)
    d[xp(N - 1), :] = last - 2.0 * h[xp(N - 1), :]
    d[xp(0), :] = first - 2.0 * h[xp(0), :]

    def back(t, nxt):
        i = N - 1 - t
        cur = (s_in[xp(i), :] + bx[xp(i), :] * first) + ex[xp(i), :] * nxt
        d[xp(i), :] = cur - 2.0 * h[xp(i), :]
        return cur

    lax.fori_loop(1, N - 1, back, last, unroll=10)

    def step(i, state):
        s, r = state
        s_out[xp(i), :] = s * iy[xp(i), :]
        return d[yp(i + 1), :] + ey[xp(i), :] * s, r + by[xp(i), :] * s

    s, r = lax.fori_loop(1, N - 1, step, (d[yp(1), :], d[yp(0), :]), unroll=10)
    send_segment(out, shares_y, my, r, s)


def final_kernel(ends, s_in, by, ey, my, shares, zb, ze, zi, ez, iz, h, out, d, t, sems):
    first, last = end_cells(ends, shares, my)
    d[xp(N - 1), :] = last
    d[xp(0), :] = first

    def back(u, nxt):
        j = N - 1 - u
        cur = (s_in[xp(j), :] + by[xp(j), :] * first) + ey[xp(j), :] * nxt
        d[xp(j), :] = cur
        return cur

    lax.fori_loop(1, N - 1, back, last, unroll=10)

    for g in range(8):
        lines = jnp.concatenate([d[yp(i), :] for i in range(4 * g, 4 * g + 4)])
        t[pl.ds(g, L, stride=8), :] = jnp.transpose(lines)

    def reduced(m):
        return (t[zp(2 * m), :] + zb[zp(m), :] * t[zp(2 * m + 1), :]) + ze[zp(m - 1), :] * t[zp(2 * m - 1), :]

    def down(q, state):
        lo, hi = state
        m = LAST - q
        next_lo = reduced(q + 1) + ez[zp(q), :] * lo
        next_hi = reduced(m - 1) + ez[zp(m), :] * hi
        t[zp(2 * q), :] = lo * iz[zp(q), :]
        t[zp(2 * m), :] = hi * iz[zp(m), :]
        return next_lo, next_hi

    lo, hi = t[zp(0), :] + zb[zp(0), :] * t[zp(1), :], reduced(LAST)
    lo, hi = lax.fori_loop(0, MID, down, (lo, hi), unroll=31)
    mid = (lo + ez[zp(MID + 1), :] * hi) * iz[zp(MID), :]
    t[zp(2 * MID), :] = mid
    t[zp(2 * MID + 2), :] = hi * iz[zp(MID + 1), :]

    def odd_back(m, below, above):
        at = zp(2 * m + 1)
        t[at, :] = (zi[zp(m), :] * t[at, :] + zb[zp(m), :] * below) + ze[zp(m), :] * above

    def up(q, state):
        lo, hi = state
        a = MID - 1 - q
        b = MID + 1 + q
        next_lo = t[zp(2 * a), :] + ez[zp(a), :] * lo
        next_hi = t[zp(2 * b), :] + ez[zp(b), :] * hi
        t[zp(2 * a), :] = next_lo
        t[zp(2 * b), :] = next_hi
        odd_back(a, next_lo, lo)
        odd_back(b - 1, hi, next_hi)
        return next_lo, next_hi

    lo, hi = lax.fori_loop(0, MID, up, (mid, mid), unroll=31)
    next_hi = t[zp(2 * LAST), :] + ez[zp(LAST), :] * hi
    t[zp(2 * LAST), :] = next_hi
    odd_back(LAST - 1, hi, next_hi)
    odd_back(LAST, next_hi, 0.0)

    copies = []
    for g in range(8):
        at = pl.ds(g * L, L)
        d[at, :] = h[at, :] + jnp.transpose(t[pl.ds(g, L, stride=8), :])
        copies.append(pltpu.make_async_copy(d.at[at, :], out.at[at, :], sems.at[g]))
        copies[g].start()
    for copy in copies:
        copy.wait()


BLOCK = (ROWS, L)
HALF = (ROWS // 2, L)
NET = (N * ROW, L)
ENDS = (N * 2, L)


def planes(*lead):
    return lead + (N, L)


def call(kernel, outs, *args, scratch=(), sems=0, hbm_in=(), hbm_out=False, flops=1000000):
    spec = {True: pl.BlockSpec(memory_space=pltpu.HBM), False: pl.BlockSpec(memory_space=pltpu.VMEM)}
    moved = 4 * sum(a.size for a in args)
    args = [
        pltpu.with_memory_space_constraint(a, pltpu.HBM if i in hbm_in else pltpu.VMEM)
        for i, a in enumerate(args)
    ]
    make = jax.ShapeDtypeStruct if hbm_out else pltpu.VMEM
    scratch_shapes = [pltpu.VMEM(s, jnp.float32) for s in scratch]
    if sems:
        scratch_shapes.append(pltpu.SemaphoreType.DMA((sems,)))
    return pl.pallas_call(
        kernel,
        out_shape=[make(s, jnp.float32) for s in outs],
        in_specs=[spec[i in hbm_in] for i in range(len(args))],
        out_specs=[spec[hbm_out]] * len(outs),
        scratch_shapes=scratch_shapes,
        compiler_params=pltpu.CompilerParams(vmem_limit_bytes=VMEM_LIMIT),
        cost_estimate=pl.CostEstimate(flops=flops, bytes_accessed=moved, transcendentals=0),
    )(*args)


def line_ends(net, axis):
    chunk = N // lax.axis_size(axis)
    got = lax.all_to_all(net.reshape(N, 1, ROW * L), axis, 0, 0, tiled=True).reshape(NET)
    (ends,) = call(functools.partial(ends_kernel, chunk), [ENDS], got, flops=100000)
    return lax.all_to_all(ends.reshape(N, 2, L), axis, 0, 0, tiled=True).reshape(ENDS)


def per_device(water_head, conductivity, recharge):
    h, k, rc = (a.reshape(ROWS, L) for a in (water_head, conductivity, recharge))
    far, near = call(
        pack_kernel, [planes(2)] * 2, water_head, conductivity, sems=4, hbm_in=(0, 1), flops=10000
    )
    count = lax.axis_size("gy")
    across = [(i, i + 1) for i in range(1, count - 1, 2)]
    far_in = lax.ppermute(far, "gy", across + [(i, j) for j, i in across])
    near_in = lax.ppermute(near, "gy", [(i, i ^ 1) for i in range(count)])
    f, bx, ex, ix, mx, by, ey, iy, my, *z = call(
        local_kernel,
        [BLOCK] * 4 + [planes(9)] + [BLOCK] * 3 + [planes(9)] + [HALF] * 5,
        h, k,
        scratch=[BLOCK] * 4,
        flops=20000000,
    )
    net, sx, shares = call(
        x_down_kernel,
        [NET, BLOCK, planes(2)],
        f, rc, bx, ex, ix, mx, far, near, far_in, near_in,
        scratch=[BLOCK],
    )
    ends = line_ends(net, "gx")
    net, sy, shares = call(
        x_up_kernel,
        [NET, BLOCK, planes(2)],
        ends, sx, bx, ex, mx, shares, h, by, ey, iy, my,
        scratch=[BLOCK],
    )
    ends = line_ends(net, "gy")
    (out,) = call(
        final_kernel, [BLOCK], ends, sy, by, ey, my, shares, *z, h, hbm_out=True, scratch=[BLOCK] * 2, sems=8
    )
    return out.reshape(water_head.shape)


def solution(mesh):
    placed = (P("gx", "gy", None),) * 3
    return jax.shard_map(
        per_device, mesh=mesh, in_specs=placed, out_specs=P("gx", "gy", None), check_vma=False
    )
```

```python
import functools

import jax
import jax.numpy as jnp
from jax import lax
from jax.experimental import pallas as pl
from jax.experimental.pallas import tpu as pltpu
from jax.sharding import PartitionSpec as P

COEF_Z = 8.0
COEF_X = 5120.0
COEF_Y = 5120.0

N = 32
L = 128
ROWS = N * N
ROW = 5
LAST = L // 2 - 1
MID = LAST // 2
VMEM_LIMIT = 24 << 20


def link(coef, one, other):
    return coef * (one * other) / (one + other)


def xp(i):
    return pl.ds(pl.multiple_of(i * N, N), N)


def yp(j):
    return pl.ds(j, N, stride=N)


def zp(z):
    return pl.ds(pl.multiple_of(z * 8, 8), 8)


def halo_planes():
    odd = lax.rem(lax.axis_index("gy"), 2)
    return (1 - odd) * (N - 1), odd * (N - 1)


def pack_kernel(h, k, far, near, sems):
    at_near, at_far = halo_planes()
    copies = [
        pltpu.make_async_copy(src.at[:, at, :], out.at[row], sems.at[2 * side + row])
        for side, (out, at) in enumerate(((far, at_far), (near, at_near)))
        for row, src in enumerate((h, k))
    ]
    for copy in copies:
        copy.start()
    for copy in copies:
        copy.wait()


def chain_step(i, state, e, b_out, e_out, i_out):
    beta, ground, a = state
    inv = 1.0 / (beta + e + ground)
    bh = beta * inv
    eh = e * inv
    b_out[xp(i), :] = bh
    e_out[xp(i), :] = eh
    i_out[xp(i), :] = inv
    return bh * e, 1.0 + eh * ground, a + bh * ground


def local_kernel(h, k, f, bx, ex, ix, mx, by, ey, iy, my, zb, ze, zi, ez, iz, wx, wy, wz, wzt):
    lane = lax.broadcasted_iota(jnp.int32, (N, L), 1)
    row = lax.broadcasted_iota(jnp.int32, (N, L), 0)
    one = jnp.ones((N, L), jnp.float32)
    coef_y = jnp.where(row < N - 1, COEF_Y, 0.0)
    coef_z = jnp.where(lane < L - 1, COEF_Z, 0.0)

    def flows(i, k0, kn, hn):
        h0 = 2.0 * h[xp(i), :]
        w = link(coef_y, k0, kn)
        wy[xp(i), :] = w
        up = w * (2.0 * hn - h0)
        total = h0 + (up - pltpu.roll(up, 1, 0))
        w = link(coef_z, k0, pltpu.roll(k0, L - 1, 1))
        wz[xp(i), :] = w
        up = w * (pltpu.roll(h0, L - 1, 1) - h0)
        f[xp(i), :] = total + (up - pltpu.roll(up, 1, 1))

    def further(ref, i):
        return ref[pl.ds(pl.multiple_of(i * N, N) + 1, N), :]

    def plane(i, k0):
        k1 = k[xp(i + 1), :]
        wx[xp(i), :] = link(COEF_X, k0, k1)
        flows(i, k0, further(k, i), further(h, i))
        return k1

    k0 = k[xp(0), :]
    k1 = lax.fori_loop(1, N - 1, plane, plane(0, k0), unroll=5)
    flows(N - 1, k1, pltpu.roll(k1, N - 1, 0), pltpu.roll(h[xp(N - 1), :], N - 1, 0))

    for g in range(8):
        wzt[pl.ds(g, L, stride=8), :] = jnp.transpose(wz[pl.ds(g * L, L), :])

    def odd_cell(m):
        w0 = wzt[zp(2 * m), :]
        w1 = wzt[zp(2 * m + 1), :]
        inv = 1.0 / (1.0 + w0 + w1)
        b = w0 * inv
        e = w1 * inv
        zb[zp(m), :] = b
        ze[zp(m), :] = e
        zi[zp(m), :] = inv
        return b, e, b * w1

    def even_cell(m, ground, past):
        inv = 1.0 / (ground + past)
        eh = past * inv
        ez[zp(m), :] = eh
        iz[zp(m), :] = inv
        return eh * ground

    def z_step(q, state):
        lo, (b0, e0, w0), o1, hi, p0, p1 = state
        lo = (1.0 + e0 + o1[0]) + even_cell(q, lo, w0)
        hi = (1.0 + p0[0] + p1[1]) + even_cell(LAST - q, hi, p0[2])
        return lo, o1, odd_cell(q + 2), hi, p1, odd_cell(LAST - 3 - q)

    def chains(i, state):
        sx, sy, sz = state
        sx = chain_step(i, sx, wx[xp(i), :], bx, ex, ix)
        sy = chain_step(i, sy, wy[yp(i), :], by, ey, iy)
        return sx, sy, z_step(i - 1, sz)

    o0, o1 = odd_cell(0), odd_cell(1)
    top, p0, p1 = odd_cell(LAST), odd_cell(LAST - 1), odd_cell(LAST - 2)
    sz = (1.0 + o0[0], o0, o1, 1.0 + top[0] + p0[1], p0, p1)
    sx, sy, sz = lax.fori_loop(
        1, N - 1, chains, ((wx[xp(0), :], one, one), (wy[yp(0), :], one, one), sz), unroll=3
    )
    close_segment(mx, sx, COEF_X * k[xp(0), :], COEF_X * k[xp(N - 1), :])
    close_segment(my, sy, COEF_Y * k[yp(0), :], COEF_Y * k[yp(N - 1), :])
    lo, (b0, e0, w0), o1, hi, p0, p1 = sz
    lo = (1.0 + e0 + o1[0]) + even_cell(MID - 1, lo, w0)
    hi = (1.0 + p0[0] + p1[1]) + even_cell(MID + 2, hi, p0[2])
    lo = lo + even_cell(MID + 1, hi, p1[2])
    iz[zp(MID), :] = 1.0 / lo


def close_segment(m, state, half0, half1):
    beta, c, a = state
    inv0 = 1.0 / (half0 + beta + a)
    wh, bh = half0 * inv0, beta * inv0
    past = wh * beta
    c = c + bh * a
    inv1 = 1.0 / (past + half1 + c)
    lh, uh = past * inv1, half1 * inv1
    for at, value in enumerate((lh * half1, wh * a + lh * c, uh * c, wh, bh, inv0, lh, uh, inv1)):
        m[at] = value


def send_segment(out, shares, m, r, s):
    s = s + m[4] * r
    for at, value in enumerate((m[0], m[1], m[2], m[3] * r + m[6] * s, m[7] * s)):
        out[pl.ds(at, N, stride=ROW), :] = value
    shares[0], shares[1] = m[5] * r, m[8] * s


def end_cells(ends, shares, m):
    before, after = ends[pl.ds(0, N, stride=2), :], ends[pl.ds(1, N, stride=2), :]
    last = shares[1] + m[6] * before + m[7] * after
    return shares[0] + m[3] * before + m[4] * last, last


def x_down_kernel(f, rc, bx, ex, ix, mx, far, near, far_in, near_in, out, s_out, shares, g):
    g[...] = f[...] + rc[...]
    at_near, at_far = halo_planes()
    for at, mine, theirs in ((at_far, far, far_in), (at_near, near, near_in)):
        w = link(COEF_Y, mine[1], theirs[1])
        g[yp(at), :] = g[yp(at), :] + 2.0 * w * (theirs[0] - mine[0])

    def step(i, state):
        s, r = state
        s_out[xp(i), :] = s * ix[xp(i), :]
        return g[xp(i + 1), :] + ex[xp(i), :] * s, r + bx[xp(i), :] * s

    s, r = lax.fori_loop(
        1, N - 1, step, (g[xp(1), :], g[xp(0), :]), unroll=5
    )
    send_segment(out, shares, mx, r, s)


def ends_kernel(chunk, net, out):
    row = lax.broadcasted_iota(jnp.int32, (N, L), 0)

    def before(v, s):
        return jnp.where(row >= s, pltpu.roll(v, s, 0), 0.0)

    def after(v, s):
        return jnp.where(row < N - s, pltpu.roll(v, N - s, 0), 0.0)

    past, g0, g1, r0, r1 = (net[pl.ds(at, N, stride=ROW), :] for at in range(ROW))
    final = row >= N - chunk
    inv_final = 1.0 / (past + g1)
    share = jnp.where(final, past * inv_final, 0.0)
    beta = before(past, chunk)
    ground = g0 + before(g1, chunk) + share * g1
    rhs = r0 + before(r1, chunk) + share * r1
    s = chunk
    while s < N:
        nxt = after(beta, s)
        inv = 1.0 / (ground + beta + nxt)
        gh, rh, lh = ground * inv, rhs * inv, beta * inv
        ground = ground + beta * before(gh, s) + nxt * after(gh, s)
        rhs = rhs + beta * before(rh, s) + nxt * after(rh, s)
        beta = beta * before(lh, s)
        s *= 2
    q = rhs / ground
    out[pl.ds(0, N, stride=2), :] = q
    out[pl.ds(1, N, stride=2), :] = jnp.where(final, (r1 + past * q) * inv_final, after(q, chunk))


def x_up_kernel(ends, s_in, bx, ex, mx, shares, h, by, ey, iy, my, out, s_out, shares_y, d):
    first, last = end_cells(ends, shares, mx)
    d[xp(N - 1), :] = last - 2.0 * h[xp(N - 1), :]
    d[xp(0), :] = first - 2.0 * h[xp(0), :]

    def back(t, nxt):
        i = N - 1 - t
        cur = (s_in[xp(i), :] + bx[xp(i), :] * first) + ex[xp(i), :] * nxt
        d[xp(i), :] = cur - 2.0 * h[xp(i), :]
        return cur

    lax.fori_loop(1, N - 1, back, last, unroll=10)

    def step(i, state):
        s, r = state
        s_out[xp(i), :] = s * iy[xp(i), :]
        return d[yp(i + 1), :] + ey[xp(i), :] * s, r + by[xp(i), :] * s

    s, r = lax.fori_loop(1, N - 1, step, (d[yp(1), :], d[yp(0), :]), unroll=10)
    send_segment(out, shares_y, my, r, s)


def final_kernel(ends, s_in, by, ey, my, shares, zb, ze, zi, ez, iz, h, out, d, t, sems):
    first, last = end_cells(ends, shares, my)
    d[xp(N - 1), :] = last
    d[xp(0), :] = first

    def back(u, nxt):
        j = N - 1 - u
        cur = (s_in[xp(j), :] + by[xp(j), :] * first) + ey[xp(j), :] * nxt
        d[xp(j), :] = cur
        return cur

    lax.fori_loop(1, N - 1, back, last, unroll=10)

    for g in range(8):
        lines = jnp.concatenate([d[yp(i), :] for i in range(4 * g, 4 * g + 4)])
        t[pl.ds(g, L, stride=8), :] = jnp.transpose(lines)

    def reduced(m):
        return (t[zp(2 * m), :] + zb[zp(m), :] * t[zp(2 * m + 1), :]) + ze[zp(m - 1), :] * t[zp(2 * m - 1), :]

    def down(q, state):
        lo, hi = state
        m = LAST - q
        next_lo = reduced(q + 1) + ez[zp(q), :] * lo
        next_hi = reduced(m - 1) + ez[zp(m), :] * hi
        t[zp(2 * q), :] = lo * iz[zp(q), :]
        t[zp(2 * m), :] = hi * iz[zp(m), :]
        return next_lo, next_hi

    lo, hi = t[zp(0), :] + zb[zp(0), :] * t[zp(1), :], reduced(LAST)
    lo, hi = lax.fori_loop(0, MID, down, (lo, hi), unroll=31)
    mid = (lo + ez[zp(MID + 1), :] * hi) * iz[zp(MID), :]
    t[zp(2 * MID), :] = mid
    t[zp(2 * MID + 2), :] = hi * iz[zp(MID + 1), :]

    def odd_back(m, below, above):
        at = zp(2 * m + 1)
        t[at, :] = (zi[zp(m), :] * t[at, :] + zb[zp(m), :] * below) + ze[zp(m), :] * above

    def up(q, state):
        lo, hi = state
        a = MID - 1 - q
        b = MID + 1 + q
        next_lo = t[zp(2 * a), :] + ez[zp(a), :] * lo
        next_hi = t[zp(2 * b), :] + ez[zp(b), :] * hi
        t[zp(2 * a), :] = next_lo
        t[zp(2 * b), :] = next_hi
        odd_back(a, next_lo, lo)
        odd_back(b - 1, hi, next_hi)
        return next_lo, next_hi

    lo, hi = lax.fori_loop(0, MID, up, (mid, mid), unroll=31)
    next_hi = t[zp(2 * LAST), :] + ez[zp(LAST), :] * hi
    t[zp(2 * LAST), :] = next_hi
    odd_back(LAST - 1, hi, next_hi)
    odd_back(LAST, next_hi, 0.0)

    copies = []
    for g in range(8):
        at = pl.ds(g * L, L)
        d[at, :] = h[at, :] + jnp.transpose(t[pl.ds(g, L, stride=8), :])
        for half in range(2):
            part = pl.ds(g * L + half * (L // 2), L // 2)
            copies.append(pltpu.make_async_copy(d.at[part, :], out.at[part, :], sems.at[2 * g + half]))
            copies[-1].start()
    for copy in copies:
        copy.wait()


BLOCK = (ROWS, L)
HALF = (ROWS // 2, L)
NET = (N * ROW, L)
ENDS = (N * 2, L)


def planes(*lead):
    return lead + (N, L)


def call(kernel, outs, *args, scratch=(), sems=0, hbm_in=(), hbm_out=False, flops=1000000):
    spec = {True: pl.BlockSpec(memory_space=pltpu.HBM), False: pl.BlockSpec(memory_space=pltpu.VMEM)}
    moved = 4 * sum(a.size for a in args)
    args = [
        pltpu.with_memory_space_constraint(a, pltpu.HBM if i in hbm_in else pltpu.VMEM)
        for i, a in enumerate(args)
    ]
    make = jax.ShapeDtypeStruct if hbm_out else pltpu.VMEM
    scratch_shapes = [pltpu.VMEM(s, jnp.float32) for s in scratch]
    if sems:
        scratch_shapes.append(pltpu.SemaphoreType.DMA((sems,)))
    return pl.pallas_call(
        kernel,
        out_shape=[make(s, jnp.float32) for s in outs],
        in_specs=[spec[i in hbm_in] for i in range(len(args))],
        out_specs=[spec[hbm_out]] * len(outs),
        scratch_shapes=scratch_shapes,
        compiler_params=pltpu.CompilerParams(vmem_limit_bytes=VMEM_LIMIT),
        cost_estimate=pl.CostEstimate(flops=flops, bytes_accessed=moved, transcendentals=0),
    )(*args)


def line_ends(net, axis):
    chunk = N // lax.axis_size(axis)
    got = lax.all_to_all(net.reshape(N, 1, ROW * L), axis, 0, 0, tiled=True).reshape(NET)
    (ends,) = call(functools.partial(ends_kernel, chunk), [ENDS], got, flops=100000)
    return lax.all_to_all(ends.reshape(N, 2, L), axis, 0, 0, tiled=True).reshape(ENDS)


def per_device(water_head, conductivity, recharge):
    h, k, rc = (a.reshape(ROWS, L) for a in (water_head, conductivity, recharge))
    far, near = call(
        pack_kernel, [planes(2)] * 2, water_head, conductivity, sems=4, hbm_in=(0, 1), flops=10000
    )
    count = lax.axis_size("gy")
    across = [(i, i + 1) for i in range(1, count - 1, 2)]
    far_in = lax.ppermute(far, "gy", across + [(i, j) for j, i in across])
    near_in = lax.ppermute(near, "gy", [(i, i ^ 1) for i in range(count)])
    f, bx, ex, ix, mx, by, ey, iy, my, *z = call(
        local_kernel,
        [BLOCK] * 4 + [planes(9)] + [BLOCK] * 3 + [planes(9)] + [HALF] * 5,
        h, k,
        scratch=[BLOCK] * 4,
        flops=20000000,
    )
    net, sx, shares = call(
        x_down_kernel,
        [NET, BLOCK, planes(2)],
        f, rc, bx, ex, ix, mx, far, near, far_in, near_in,
        scratch=[BLOCK],
    )
    ends = line_ends(net, "gx")
    net, sy, shares = call(
        x_up_kernel,
        [NET, BLOCK, planes(2)],
        ends, sx, bx, ex, mx, shares, h, by, ey, iy, my,
        scratch=[BLOCK],
    )
    ends = line_ends(net, "gy")
    (out,) = call(
        final_kernel, [BLOCK], ends, sy, by, ey, my, shares, *z, h, hbm_out=True, scratch=[BLOCK] * 2, sems=16
    )
    return out.reshape(water_head.shape)


def solution(mesh):
    placed = (P("gx", "gy", None),) * 3
    return jax.shard_map(
        per_device, mesh=mesh, in_specs=placed, out_specs=P("gx", "gy", None), check_vma=False
    )
```

```python
import functools

import jax
import jax.numpy as jnp
from jax import lax
from jax.experimental import pallas as pl
from jax.experimental.pallas import tpu as pltpu
from jax.sharding import PartitionSpec as P

COEF_Z = 8.0
COEF_X = 5120.0
COEF_Y = 5120.0

N = 32
L = 128
ROWS = N * N
ROW = 5
LAST = L // 2 - 1
MID = LAST // 2
VMEM_LIMIT = 24 << 20


def link(coef, one, other):
    return coef * (one * other) / (one + other)


def xp(i):
    return pl.ds(pl.multiple_of(i * N, N), N)


def yp(j):
    return pl.ds(j, N, stride=N)


def zp(z):
    return pl.ds(pl.multiple_of(z * 8, 8), 8)


def halo_planes():
    odd = lax.rem(lax.axis_index("gy"), 2)
    return (1 - odd) * (N - 1), odd * (N - 1)


def pack_kernel(h, k, far, near, sems):
    at_near, at_far = halo_planes()
    copies = [
        pltpu.make_async_copy(src.at[:, at, :], out.at[row], sems.at[2 * side + row])
        for side, (out, at) in enumerate(((far, at_far), (near, at_near)))
        for row, src in enumerate((h, k))
    ]
    for copy in copies:
        copy.start()
    for copy in copies:
        copy.wait()


def chain_step(i, state, e, b_out, e_out, i_out):
    beta, ground, a = state
    inv = 1.0 / (beta + e + ground)
    bh = beta * inv
    eh = e * inv
    b_out[xp(i), :] = bh
    e_out[xp(i), :] = eh
    i_out[xp(i), :] = inv
    return bh * e, 1.0 + eh * ground, a + bh * ground


def local_kernel(h, k, f, bx, ex, ix, mx, by, ey, iy, my, zb, ze, zi, ez, iz, wx, wy, wz, wzt):
    lane = lax.broadcasted_iota(jnp.int32, (N, L), 1)
    row = lax.broadcasted_iota(jnp.int32, (N, L), 0)
    one = jnp.ones((N, L), jnp.float32)
    coef_y = jnp.where(row < N - 1, COEF_Y, 0.0)
    coef_z = jnp.where(lane < L - 1, COEF_Z, 0.0)

    def flows(i, k0, kn, hn):
        h0 = 2.0 * h[xp(i), :]
        w = link(coef_y, k0, kn)
        wy[xp(i), :] = w
        up = w * (2.0 * hn - h0)
        total = h0 + (up - pltpu.roll(up, 1, 0))
        w = link(coef_z, k0, pltpu.roll(k0, L - 1, 1))
        wz[xp(i), :] = w
        up = w * (pltpu.roll(h0, L - 1, 1) - h0)
        f[xp(i), :] = total + (up - pltpu.roll(up, 1, 1))

    def further(ref, i):
        return ref[pl.ds(pl.multiple_of(i * N, N) + 1, N), :]

    def plane(i, k0):
        k1 = k[xp(i + 1), :]
        wx[xp(i), :] = link(COEF_X, k0, k1)
        flows(i, k0, further(k, i), further(h, i))
        return k1

    k0 = k[xp(0), :]
    k1 = lax.fori_loop(1, N - 1, plane, plane(0, k0), unroll=5)
    flows(N - 1, k1, pltpu.roll(k1, N - 1, 0), pltpu.roll(h[xp(N - 1), :], N - 1, 0))

    for g in range(8):
        wzt[pl.ds(g, L, stride=8), :] = jnp.transpose(wz[pl.ds(g * L, L), :])

    def odd_cell(m):
        w0 = wzt[zp(2 * m), :]
        w1 = wzt[zp(2 * m + 1), :]
        inv = 1.0 / (1.0 + w0 + w1)
        b = w0 * inv
        e = w1 * inv
        zb[zp(m), :] = b
        ze[zp(m), :] = e
        zi[zp(m), :] = inv
        return b, e, b * w1

    def even_cell(m, ground, past):
        inv = 1.0 / (ground + past)
        eh = past * inv
        ez[zp(m), :] = eh
        iz[zp(m), :] = inv
        return eh * ground

    def z_step(q, state):
        lo, (b0, e0, w0), o1, hi, p0, p1 = state
        lo = (1.0 + e0 + o1[0]) + even_cell(q, lo, w0)
        hi = (1.0 + p0[0] + p1[1]) + even_cell(LAST - q, hi, p0[2])
        return lo, o1, odd_cell(q + 2), hi, p1, odd_cell(LAST - 3 - q)

    def chains(i, state):
        sx, sy, sz = state
        sx = chain_step(i, sx, wx[xp(i), :], bx, ex, ix)
        sy = chain_step(i, sy, wy[yp(i), :], by, ey, iy)
        return sx, sy, z_step(i - 1, sz)

    o0, o1 = odd_cell(0), odd_cell(1)
    top, p0, p1 = odd_cell(LAST), odd_cell(LAST - 1), odd_cell(LAST - 2)
    sz = (1.0 + o0[0], o0, o1, 1.0 + top[0] + p0[1], p0, p1)
    sx, sy, sz = lax.fori_loop(
        1, N - 1, chains, ((wx[xp(0), :], one, one), (wy[yp(0), :], one, one), sz), unroll=3
    )
    close_segment(mx, sx, COEF_X * k[xp(0), :], COEF_X * k[xp(N - 1), :])
    close_segment(my, sy, COEF_Y * k[yp(0), :], COEF_Y * k[yp(N - 1), :])
    lo, (b0, e0, w0), o1, hi, p0, p1 = sz
    lo = (1.0 + e0 + o1[0]) + even_cell(MID - 1, lo, w0)
    hi = (1.0 + p0[0] + p1[1]) + even_cell(MID + 2, hi, p0[2])
    lo = lo + even_cell(MID + 1, hi, p1[2])
    iz[zp(MID), :] = 1.0 / lo


def close_segment(m, state, half0, half1):
    beta, c, a = state
    inv0 = 1.0 / (half0 + beta + a)
    wh, bh = half0 * inv0, beta * inv0
    past = wh * beta
    c = c + bh * a
    inv1 = 1.0 / (past + half1 + c)
    lh, uh = past * inv1, half1 * inv1
    for at, value in enumerate((lh * half1, wh * a + lh * c, uh * c, wh, bh, inv0, lh, uh, inv1)):
        m[at] = value


def send_segment(out, shares, m, r, s):
    s = s + m[4] * r
    for at, value in enumerate((m[0], m[1], m[2], m[3] * r + m[6] * s, m[7] * s)):
        out[pl.ds(at, N, stride=ROW), :] = value
    shares[0], shares[1] = m[5] * r, m[8] * s


def end_cells(ends, shares, m):
    before, after = ends[pl.ds(0, N, stride=2), :], ends[pl.ds(1, N, stride=2), :]
    last = shares[1] + m[6] * before + m[7] * after
    return shares[0] + m[3] * before + m[4] * last, last


def x_down_kernel(f, rc, bx, ex, ix, mx, far, near, far_in, near_in, out, s_out, shares, g):
    g[...] = f[...] + rc[...]
    at_near, at_far = halo_planes()
    for at, mine, theirs in ((at_far, far, far_in), (at_near, near, near_in)):
        w = link(COEF_Y, mine[1], theirs[1])
        g[yp(at), :] = g[yp(at), :] + 2.0 * w * (theirs[0] - mine[0])

    def step(i, state):
        s, r = state
        s_out[xp(i), :] = s * ix[xp(i), :]
        return g[xp(i + 1), :] + ex[xp(i), :] * s, r + bx[xp(i), :] * s

    s, r = lax.fori_loop(
        1, N - 1, step, (g[xp(1), :], g[xp(0), :]), unroll=5
    )
    send_segment(out, shares, mx, r, s)


def ends_kernel(chunk, net, out):
    row = lax.broadcasted_iota(jnp.int32, (N, L), 0)

    def before(v, s):
        return jnp.where(row >= s, pltpu.roll(v, s, 0), 0.0)

    def after(v, s):
        return jnp.where(row < N - s, pltpu.roll(v, N - s, 0), 0.0)

    past, g0, g1, r0, r1 = (net[pl.ds(at, N, stride=ROW), :] for at in range(ROW))
    final = row >= N - chunk
    inv_final = 1.0 / (past + g1)
    share = jnp.where(final, past * inv_final, 0.0)
    beta = before(past, chunk)
    ground = g0 + before(g1, chunk) + share * g1
    rhs = r0 + before(r1, chunk) + share * r1
    s = chunk
    while s < N:
        nxt = after(beta, s)
        inv = 1.0 / (ground + beta + nxt)
        gh, rh, lh = ground * inv, rhs * inv, beta * inv
        ground = ground + beta * before(gh, s) + nxt * after(gh, s)
        rhs = rhs + beta * before(rh, s) + nxt * after(rh, s)
        beta = beta * before(lh, s)
        s *= 2
    q = rhs / ground
    out[pl.ds(0, N, stride=2), :] = q
    out[pl.ds(1, N, stride=2), :] = jnp.where(final, (r1 + past * q) * inv_final, after(q, chunk))


def x_up_kernel(ends, s_in, bx, ex, mx, shares, h, by, ey, iy, my, out, s_out, shares_y, d):
    first, last = end_cells(ends, shares, mx)
    d[xp(N - 1), :] = last - 2.0 * h[xp(N - 1), :]
    d[xp(0), :] = first - 2.0 * h[xp(0), :]

    def back(t, nxt):
        i = N - 1 - t
        cur = (s_in[xp(i), :] + bx[xp(i), :] * first) + ex[xp(i), :] * nxt
        d[xp(i), :] = cur - 2.0 * h[xp(i), :]
        return cur

    lax.fori_loop(1, N - 1, back, last, unroll=10)

    def step(i, state):
        s, r = state
        s_out[xp(i), :] = s * iy[xp(i), :]
        return d[yp(i + 1), :] + ey[xp(i), :] * s, r + by[xp(i), :] * s

    s, r = lax.fori_loop(1, N - 1, step, (d[yp(1), :], d[yp(0), :]), unroll=10)
    send_segment(out, shares_y, my, r, s)


def final_kernel(ends, s_in, by, ey, my, shares, zb, ze, zi, ez, iz, h, out, d, t, sems):
    first, last = end_cells(ends, shares, my)
    d[xp(N - 1), :] = last
    d[xp(0), :] = first

    def back(u, nxt):
        j = N - 1 - u
        cur = (s_in[xp(j), :] + by[xp(j), :] * first) + ey[xp(j), :] * nxt
        d[xp(j), :] = cur
        return cur

    lax.fori_loop(1, N - 1, back, last, unroll=10)

    for g in range(8):
        lines = jnp.concatenate([d[yp(i), :] for i in range(4 * g, 4 * g + 4)])
        t[pl.ds(g, L, stride=8), :] = jnp.transpose(lines)

    def reduced(m):
        return (t[zp(2 * m), :] + zb[zp(m), :] * t[zp(2 * m + 1), :]) + ze[zp(m - 1), :] * t[zp(2 * m - 1), :]

    def down(q, state):
        lo, hi = state
        m = LAST - q
        next_lo = reduced(q + 1) + ez[zp(q), :] * lo
        next_hi = reduced(m - 1) + ez[zp(m), :] * hi
        t[zp(2 * q), :] = lo * iz[zp(q), :]
        t[zp(2 * m), :] = hi * iz[zp(m), :]
        return next_lo, next_hi

    lo, hi = t[zp(0), :] + zb[zp(0), :] * t[zp(1), :], reduced(LAST)
    lo, hi = lax.fori_loop(0, MID, down, (lo, hi), unroll=31)
    mid = (lo + ez[zp(MID + 1), :] * hi) * iz[zp(MID), :]
    t[zp(2 * MID), :] = mid
    t[zp(2 * MID + 2), :] = hi * iz[zp(MID + 1), :]

    def odd_back(m, below, above):
        at = zp(2 * m + 1)
        t[at, :] = (zi[zp(m), :] * t[at, :] + zb[zp(m), :] * below) + ze[zp(m), :] * above

    def up(q, state):
        lo, hi = state
        a = MID - 1 - q
        b = MID + 1 + q
        next_lo = t[zp(2 * a), :] + ez[zp(a), :] * lo
        next_hi = t[zp(2 * b), :] + ez[zp(b), :] * hi
        t[zp(2 * a), :] = next_lo
        t[zp(2 * b), :] = next_hi
        odd_back(a, next_lo, lo)
        odd_back(b - 1, hi, next_hi)
        return next_lo, next_hi

    lo, hi = lax.fori_loop(0, MID, up, (mid, mid), unroll=31)
    next_hi = t[zp(2 * LAST), :] + ez[zp(LAST), :] * hi
    t[zp(2 * LAST), :] = next_hi
    odd_back(LAST - 1, hi, next_hi)
    odd_back(LAST, next_hi, 0.0)

    copies = []
    for g in range(8):
        at = pl.ds(g * L, L)
        d[at, :] = h[at, :] + jnp.transpose(t[pl.ds(g, L, stride=8), :])
        if g % 2:
            part = pl.ds((g - 1) * L, 2 * L)
            copies.append(pltpu.make_async_copy(d.at[part, :], out.at[part, :], sems.at[g // 2]))
            copies[-1].start()
    for copy in copies:
        copy.wait()


BLOCK = (ROWS, L)
HALF = (ROWS // 2, L)
NET = (N * ROW, L)
ENDS = (N * 2, L)


def planes(*lead):
    return lead + (N, L)


def call(kernel, outs, *args, scratch=(), sems=0, hbm_in=(), hbm_out=False, flops=1000000):
    spec = {True: pl.BlockSpec(memory_space=pltpu.HBM), False: pl.BlockSpec(memory_space=pltpu.VMEM)}
    moved = 4 * sum(a.size for a in args)
    args = [
        pltpu.with_memory_space_constraint(a, pltpu.HBM if i in hbm_in else pltpu.VMEM)
        for i, a in enumerate(args)
    ]
    make = jax.ShapeDtypeStruct if hbm_out else pltpu.VMEM
    scratch_shapes = [pltpu.VMEM(s, jnp.float32) for s in scratch]
    if sems:
        scratch_shapes.append(pltpu.SemaphoreType.DMA((sems,)))
    return pl.pallas_call(
        kernel,
        out_shape=[make(s, jnp.float32) for s in outs],
        in_specs=[spec[i in hbm_in] for i in range(len(args))],
        out_specs=[spec[hbm_out]] * len(outs),
        scratch_shapes=scratch_shapes,
        compiler_params=pltpu.CompilerParams(vmem_limit_bytes=VMEM_LIMIT),
        cost_estimate=pl.CostEstimate(flops=flops, bytes_accessed=moved, transcendentals=0),
    )(*args)


def line_ends(net, axis):
    chunk = N // lax.axis_size(axis)
    got = lax.all_to_all(net.reshape(N, 1, ROW * L), axis, 0, 0, tiled=True).reshape(NET)
    (ends,) = call(functools.partial(ends_kernel, chunk), [ENDS], got, flops=100000)
    return lax.all_to_all(ends.reshape(N, 2, L), axis, 0, 0, tiled=True).reshape(ENDS)


def per_device(water_head, conductivity, recharge):
    h, k, rc = (a.reshape(ROWS, L) for a in (water_head, conductivity, recharge))
    far, near = call(
        pack_kernel, [planes(2)] * 2, water_head, conductivity, sems=4, hbm_in=(0, 1), flops=10000
    )
    count = lax.axis_size("gy")
    across = [(i, i + 1) for i in range(1, count - 1, 2)]
    far_in = lax.ppermute(far, "gy", across + [(i, j) for j, i in across])
    near_in = lax.ppermute(near, "gy", [(i, i ^ 1) for i in range(count)])
    f, bx, ex, ix, mx, by, ey, iy, my, *z = call(
        local_kernel,
        [BLOCK] * 4 + [planes(9)] + [BLOCK] * 3 + [planes(9)] + [HALF] * 5,
        h, k,
        scratch=[BLOCK] * 4,
        flops=20000000,
    )
    net, sx, shares = call(
        x_down_kernel,
        [NET, BLOCK, planes(2)],
        f, rc, bx, ex, ix, mx, far, near, far_in, near_in,
        scratch=[BLOCK],
    )
    ends = line_ends(net, "gx")
    net, sy, shares = call(
        x_up_kernel,
        [NET, BLOCK, planes(2)],
        ends, sx, bx, ex, mx, shares, h, by, ey, iy, my,
        scratch=[BLOCK],
    )
    ends = line_ends(net, "gy")
    (out,) = call(
        final_kernel, [BLOCK], ends, sy, by, ey, my, shares, *z, h, hbm_out=True, scratch=[BLOCK] * 2, sems=4
    )
    return out.reshape(water_head.shape)


def solution(mesh):
    placed = (P("gx", "gy", None),) * 3
    return jax.shard_map(
        per_device, mesh=mesh, in_specs=placed, out_specs=P("gx", "gy", None), check_vma=False
    )
```
